256 devices in a mesh: dp: 32 (over x, z), frame: 8 (over y, core).
Axes of the slice: x: 4, y: 4, z: 8, core: 2. Of those that a mesh axis runs over, the one named last changes fastest.
Arguments:
- features: bfloat16 [32, 16, 32, 64, 128], P('dp', 'frame'), may hold values from -6 to 6
- vis_block: int32 [32, 16, 16, 2], P('dp', None, 'frame'), may hold values from 0 to 31
- vis_count: int32 [32, 16, 16], P('dp', None, 'frame'), may hold values from 1 to 2
- query_frame: int32 [32, 256], P('dp'), may hold values from 0 to 15
- query_block: int32 [32, 256], P('dp'), may hold values from 0 to 31
- query_cell: int32 [32, 256], P('dp'), may hold values from 0 to 63
- cotangent: bfloat16 [32, 4, 256, 16], P('dp', None, 'frame')
- w_in: bfloat16 [128, 384], replicated, may hold values from -0.5 to 0.5
- gain: float32 [384], replicated, may hold values from 0.1 to 1.9
- w_qkv: bfloat16 [384, 1152], replicated, may hold values from -0.3125 to 0.3125
- w_out: bfloat16 [384, 384], replicated, may hold values from -0.3125 to 0.3125
- w_head: bfloat16 [4, 384], replicated, may hold values from -0.3125 to 0.3125
Outputs:
- grad_in: float32 [128, 384], replicated
- grad_gain: float32 [384], replicated
- grad_qkv: float32 [384, 1152], replicated
- grad_out: float32 [384, 384], replicated
- grad_head: float32 [4, 384], replicated
The draws below stay inside these ranges and needn't reach their ends.
Inputs may be any that keep to these rules, and one draw needn't show every extreme that they name: vis_count counts the leading visible slots of vis_block.
All inputs are finite; a program needn't handle non-finite values.
Results may differ from the reference program's by a relative error of at most 0.012.
Values may be sent and summed in bfloat16 or wider, within the bound.
No kernel may reach another device: no remote copies, remote signals or barrier semaphores. Data moves between devices by JAX's collectives and lax.ppermute only.
A program may use at most 64 MiB of HBM per device.

```python
import math
import jax
import jax.numpy as jnp
from jax import lax

C = 128
HID = 384
HEADS = 8
FRAMES = 16
P_SIZE = 64
KB = 2
CORR = 128
OUTD = 4
TG = 16
NB = 32
GROUPS = 16
TRACKS = 256
CLIPS = 32


def draw_cotangent(key, part):
    first = jax.random.fold_in(jax.random.fold_in(key, 17), 0)
    shape = (CLIPS, OUTD, TRACKS, FRAMES)
    rising = 1.0 + 2.0 * jnp.arange(CLIPS, dtype=jnp.float32) / max(CLIPS - 1, 1)
    rising = rising[:, None, None, None]
    base = jax.random.normal(first, shape, jnp.float32)
    factor = 1.0 / math.sqrt(CLIPS * TRACKS * FRAMES)
    return (base * rising * factor).astype(jnp.bfloat16)


def plant(result, key, low, high):
    shape = result.shape
    index_at = [jax.random.randint(jax.random.fold_in(key, axis), (), 0, shape[axis]) for axis in range(len(shape))]
    result = result.at[tuple(index_at)].set(low)
    longest = shape.index(max(shape))
    index_at[longest] = (index_at[longest] + 1) % shape[longest]
    return result.at[tuple(index_at)].set(high)


def block_levels(key, extent, shards, smallest, high):
    def one(dim, shards_of):
        draws = jax.random.uniform(jax.random.fold_in(jax.random.fold_in(key, 6), dim), (shards_of,), jnp.float32, smallest / len(shards), high / len(shards))
        return jnp.repeat(jnp.exp(draws), extent[dim] // shards_of).reshape((-1,) + (1,) * (len(extent) - dim - 1))

    level = one(*shards[0])
    for cut in shards[1:]:
        level = level * one(*cut)
    return level


def gaussian(key, dims, scale, limit, cuts=(), kind=jnp.bfloat16):
    loudness = block_levels(key, dims, cuts, -0.22, 0.18) if cuts else 1.0
    array = jax.random.normal(key, dims, jnp.float32) * scale * loudness
    return jnp.minimum(jnp.maximum(array, -limit), limit).astype(kind)


def setup_inputs(seed: int = 0) -> dict:
    key_of = jax.random.split(jax.random.key(seed), 13)
    features = gaussian(key_of[0], (CLIPS, FRAMES, NB, P_SIZE, C), 1.0, 6.0, ((0, 32), (1, 8)))
    vis_block = plant(jax.random.randint(key_of[1], (CLIPS, GROUPS, FRAMES, KB), 0, NB), jax.random.fold_in(key_of[1], 1), 0, NB - 1).astype(jnp.int32)
    vis_count = plant(jax.random.randint(key_of[2], (CLIPS, GROUPS, FRAMES), 1, KB + 1), jax.random.fold_in(key_of[2], 1), 1, KB).astype(jnp.int32)
    query_frame = plant(jax.random.randint(key_of[3], (CLIPS, TRACKS), 0, FRAMES), jax.random.fold_in(key_of[3], 1), 0, FRAMES - 1).astype(jnp.int32)
    query_block = plant(jax.random.randint(key_of[4], (CLIPS, TRACKS), 0, NB), jax.random.fold_in(key_of[4], 1), 0, NB - 1).astype(jnp.int32)
    query_cell = plant(jax.random.randint(key_of[5], (CLIPS, TRACKS), 0, P_SIZE), jax.random.fold_in(key_of[5], 1), 0, P_SIZE - 1).astype(jnp.int32)
    cotangent = draw_cotangent(jax.random.fold_in(key_of[12], 71), 0)
    w_in = gaussian(key_of[7], (CORR, HID), CORR ** -0.5, 0.5)
    gain = jnp.clip(1.0 + 0.18 * jax.random.normal(key_of[8], (HID,), jnp.float32), 0.1, 1.9)
    w_qkv = gaussian(key_of[9], (HID, 3 * HID), HID ** -0.5, 0.3125)
    w_out = gaussian(key_of[10], (HID, HID), HID ** -0.5, 0.3125)
    w_head = gaussian(key_of[11], (OUTD, HID), HID ** -0.5, 0.3125)
    return {"features": features, "vis_block": vis_block, "vis_count": vis_count, "query_frame": query_frame, "query_block": query_block, "query_cell": query_cell, "cotangent": cotangent, "w_in": w_in, "gain": gain, "w_qkv": w_qkv, "w_out": w_out, "w_head": w_head}


def attend(query, keys, values):
    scale = query.shape[-1] ** (-0.5)
    scores = jnp.einsum('nfhd,nghd->nhfg', query.astype(jnp.float32), keys.astype(jnp.float32)) * scale
    probs = jax.nn.softmax(scores, axis=-1).astype(jnp.bfloat16)
    probs = lax.optimization_barrier(probs)
    mixed = jnp.einsum('nhfg,nghd->nfhd', probs.astype(jnp.float32), values.astype(jnp.float32))
    return mixed.astype(jnp.bfloat16)

def local_grads(corr, cot, w_in, gain, w_qkv, w_out, w_head):
    tracks, frames, width = corr.shape
    total = tracks * frames
    hid = w_in.shape[1]
    head_size = hid // HEADS
    rows = corr.reshape(total, width)
    x_zero = jnp.dot(rows, w_in, preferred_element_type=jnp.float32)
    centred = x_zero - lax.optimization_barrier(jnp.mean(x_zero, axis=-1, keepdims=True))
    inv_std = lax.rsqrt(lax.optimization_barrier(jnp.mean(centred * centred, axis=-1, keepdims=True)) + 1e-05)
    normed = centred * inv_std
    hidden = (normed * gain).astype(jnp.bfloat16)
    qkv = jnp.dot(hidden, w_qkv, preferred_element_type=jnp.float32).astype(jnp.bfloat16)
    split = qkv.reshape(tracks, frames, 3, HEADS, head_size)
    mixed, backward = jax.vjp(attend, split[:, :, 0], split[:, :, 1], split[:, :, 2])
    mixed = mixed.reshape(total, hid)
    y_out = (x_zero + jnp.dot(mixed, w_out, preferred_element_type=jnp.float32)).astype(jnp.bfloat16)
    ct_rows = cot.reshape(cot.shape[0], total)
    g_head = jnp.dot(ct_rows, y_out, preferred_element_type=jnp.float32)
    d_y = jnp.dot(ct_rows.T, w_head, preferred_element_type=jnp.float32)
    d_y16 = d_y.astype(jnp.bfloat16)
    g_out = jnp.dot(mixed.T, d_y16, preferred_element_type=jnp.float32)
    d_mixed = jnp.dot(d_y16, w_out.T, preferred_element_type=jnp.float32).astype(jnp.bfloat16)
    d_q, d_k, d_v = backward(d_mixed.reshape(tracks, frames, HEADS, head_size))
    d_qkv = jnp.stack([d_q, d_k, d_v], axis=2).reshape(total, 3 * hid)
    g_qkv = jnp.dot(hidden.T, d_qkv, preferred_element_type=jnp.float32)
    d_hidden = jnp.dot(d_qkv, w_qkv.T, preferred_element_type=jnp.float32)
    g_gain = lax.optimization_barrier(jnp.sum(d_hidden * normed, axis=0))
    d_norm = d_hidden * gain
    d_x = inv_std * (d_norm - lax.optimization_barrier(jnp.mean(d_norm, axis=-1, keepdims=True)) - normed * lax.optimization_barrier(jnp.mean(d_norm * normed, axis=-1, keepdims=True))) + d_y
    d_x16 = d_x.astype(jnp.bfloat16)
    g_in = jnp.dot(rows.T, d_x16, preferred_element_type=jnp.float32)
    return (g_in, g_gain, g_qkv, g_out, g_head)

def correlate(feats, blocks, counts, q_frame, q_block, q_cell):
    query = feats[q_frame, q_block, q_cell]
    frame_ids = jnp.arange(FRAMES, dtype=jnp.int32)[None, :, None]
    patches = feats[frame_ids, blocks]
    live = jnp.arange(KB, dtype=jnp.int32)[None, None, :] < counts[:, :, None]
    patches = jnp.where(live[..., None, None], patches, jnp.zeros((), jnp.bfloat16))
    corr = jnp.einsum('gtc,gfkpc->gtfkp', query.reshape(GROUPS, TG, C).astype(jnp.float32), patches.astype(jnp.float32))
    corr = (corr * C ** (-0.5)).astype(jnp.bfloat16)
    return corr.reshape(TRACKS, FRAMES, KB * P_SIZE)

def reference(features, vis_block, vis_count, query_frame, query_block, query_cell, cotangent, w_in, gain, w_qkv, w_out, w_head):

    def per_clip(total, items):
        feats, blocks, counts, q_frame, q_block, q_cell, cot = items
        corr = correlate(feats, blocks, counts, q_frame, q_block, q_cell)
        grads = local_grads(corr, cot, w_in, gain, w_qkv, w_out, w_head)
        return (jax.tree.map(lambda a, b: a + b, total, grads), None)
    zeros = (jnp.zeros((KB * P_SIZE, HID), jnp.float32), jnp.zeros((HID,), jnp.float32), jnp.zeros((HID, 3 * HID), jnp.float32), jnp.zeros((HID, HID), jnp.float32), jnp.zeros((OUTD, HID), jnp.float32))
    summed, _ = lax.scan(per_clip, zeros, (features, vis_block, vis_count, query_frame, query_block, query_cell, cotangent))
    return (summed[0], summed[1], summed[2], summed[3], summed[4])
```

```python
import jax
import jax.numpy as jnp
from jax import lax
from jax.experimental import pallas as pl
from jax.experimental.pallas import tpu as pltpu
from jax.sharding import PartitionSpec as P

HEADS = 8
SIZE = 48
HID = 384
TOK = 512
ROWS = 5120
F32 = jnp.float32
BF16 = jnp.bfloat16


def dot(left, right, dims=((1,), (0,))):
    return lax.dot_general(left, right, (dims, ((), ())), preferred_element_type=F32)


NT = ((1,), (1,))
TN = ((0,), (0,))


def token_kernel(
    pat_ref,
    qry_ref,
    ct_ref,
    w_in_t,
    gain_ref,
    w_qkv_t,
    w_qkv,
    w_out_t,
    w_out,
    w_head,
    out_ref,
    corr32,
    corr16,
    x_zero,
    normed,
    hidden,
    qkv,
    mixed,
    d_y,
    d_y16,
    d_mixed,
    d_qkv,
    inv_ref,
):
    query = jnp.sum(qry_ref[...].astype(F32), axis=0).astype(BF16)
    scale = 128 ** (-0.5)
    for g in range(2):
        for s in range(8):
            part = dot(query[g * 16 : g * 16 + 16], pat_ref[s, g * 256 : g * 256 + 256], NT) * scale
            for half in range(2):
                for fr in range(2):
                    row = (g * 2 + half) * 128 + (s * 2 + fr) * 8
                    corr32[row : row + 8, :] = part[half * 8 : half * 8 + 8, fr * 128 : fr * 128 + 128]
    corr16[...] = corr32[...].astype(BF16)

    ct = ct_ref[...]
    for c in range(2):
        cols = slice(c * 256, c * 256 + 256)
        x0 = dot(w_in_t[...], corr16[cols, :], NT)
        x_zero[:, cols] = x0
        mean = jnp.mean(x0, axis=0, keepdims=True)
        centred = x0 - mean
        inv = lax.rsqrt(jnp.mean(centred * centred, axis=0, keepdims=True) + 1e-05)
        nrm = centred * inv
        inv_ref[:, cols] = jnp.broadcast_to(inv, (8, 256))
        normed[:, cols] = nrm
        hid = (nrm * gain_ref[:, :1]).astype(BF16)
        hidden[:, cols] = hid
        for r in range(3):
            rows = slice(r * 384, r * 384 + 384)
            qkv[rows, cols] = dot(w_qkv_t[rows, :], hid).astype(BF16)
        dy = dot(w_head[...], ct[:, cols], TN)
        d_y[:, cols] = dy
        dy16 = dy.astype(BF16)
        d_y16[:, cols] = dy16
        d_mixed[:, cols] = dot(w_out[...], dy16).astype(BF16)

    own = (
        lax.broadcasted_iota(jnp.int32, (8, 128), 0)
        == lax.broadcasted_iota(jnp.int32, (8, 128), 1) % 8
    ).astype(F32)
    a_scale = SIZE ** (-0.5)

    def block(b, carry):
        cols = pl.ds(pl.multiple_of(b * 128, 128), 128)
        for h in range(HEADS):
            rq = slice(h * SIZE, h * SIZE + SIZE)
            rk = slice(HID + h * SIZE, HID + h * SIZE + SIZE)
            rv = slice(2 * HID + h * SIZE, 2 * HID + h * SIZE + SIZE)
            q_t, k_t, v_t = qkv[rq, cols], qkv[rk, cols], qkv[rv, cols]
            d_a = d_mixed[rq, cols]
            score = dot(k_t, q_t, TN).reshape(16, 8, 128) * a_scale
            expo = jnp.exp(score - jnp.max(score, axis=0, keepdims=True))
            prob = expo * (own / jnp.sum(expo, axis=0))[None]
            prob16 = prob.reshape(128, 128).astype(BF16)
            mixed[rq, cols] = dot(v_t, prob16).astype(BF16)
            d_p = dot(v_t, d_a, TN).astype(BF16).astype(F32).reshape(16, 8, 128)
            inner = jnp.sum(d_p * prob, axis=0, keepdims=True)
            d_s = (prob * (d_p - inner) * a_scale).reshape(128, 128).astype(BF16)
            d_qkv[rq, cols] = dot(k_t, d_s).astype(BF16)
            d_qkv[rk, cols] = dot(q_t, d_s, NT).astype(BF16)
            d_qkv[rv, cols] = dot(d_a, prob16, NT).astype(BF16)
        return carry

    lax.fori_loop(0, 4, block, 0)

    head = jnp.zeros((16, HID), F32)
    gain_sum = jnp.zeros((HID, 128), F32)
    g_in = jnp.zeros((128, HID), F32)
    for c in range(2):
        cols = slice(c * 256, c * 256 + 256)
        y16 = (x_zero[:, cols] + dot(w_out_t[...], mixed[:, cols])).astype(BF16)
        head = head + dot(ct[:, cols], y16, NT)
        dh = dot(w_qkv[...], d_qkv[:, cols])
        nrm = normed[:, cols]
        prod = dh * nrm
        gain_sum = gain_sum + prod[:, :128] + prod[:, 128:]
        gain = gain_ref[:, :1]
        dn = dh * gain
        m_one = jnp.mean(dn, axis=0, keepdims=True)
        m_two = jnp.mean(dn * nrm, axis=0, keepdims=True)
        dx = inv_ref[:1, cols] * (dn - m_one - nrm * m_two) + d_y[:, cols]
        g_in = g_in + dot(corr16[cols, :], dx.astype(BF16), ((0,), (1,)))
    for j in range(9):
        part = dot(hidden[...], d_qkv[j * 128 : j * 128 + 128, :], NT)
        out_ref[j * 384 : j * 384 + 384, :] = part.astype(BF16)
    for j in range(3):
        part = dot(mixed[...], d_y16[j * 128 : j * 128 + 128, :], NT)
        out_ref[3456 + j * 384 : 3456 + j * 384 + 384, :] = part.astype(BF16)
    gain_row = jnp.sum(gain_sum.T, axis=0, keepdims=True)
    at_four = lax.broadcasted_iota(jnp.int32, (16, HID), 0) == 4
    head = jnp.where(at_four, jnp.broadcast_to(gain_row, (16, HID)), head)
    for j in range(3):
        lanes = slice(j * 128, j * 128 + 128)
        out_ref[4608 + j * 128 : 4736 + j * 128, :] = g_in[:, lanes].astype(BF16)
        out_ref[4992 + j * 16 : 5008 + j * 16, :] = head[:, lanes].astype(BF16)
    out_ref[5040:ROWS, :] = jnp.zeros((ROWS - 5040, 128), BF16)


def token_grads(pat, qry, ct, w_in_t, gain, w_qkv_t, w_qkv, w_out_t, w_out, w_head):
    vm = pl.BlockSpec(memory_space=pltpu.VMEM)
    return pl.pallas_call(
        token_kernel,
        out_shape=jax.ShapeDtypeStruct((ROWS, 128), BF16),
        in_specs=[vm] * 10,
        out_specs=vm,
        scratch_shapes=[
            pltpu.VMEM((TOK, 128), F32),
            pltpu.VMEM((TOK, 128), BF16),
            pltpu.VMEM((HID, TOK), F32),
            pltpu.VMEM((HID, TOK), F32),
            pltpu.VMEM((HID, TOK), BF16),
            pltpu.VMEM((3 * HID, TOK), BF16),
            pltpu.VMEM((HID, TOK), BF16),
            pltpu.VMEM((HID, TOK), F32),
            pltpu.VMEM((HID, TOK), BF16),
            pltpu.VMEM((HID, TOK), BF16),
            pltpu.VMEM((3 * HID, TOK), BF16),
            pltpu.VMEM((8, TOK), F32),
        ],
        name="token_grads",
    )(pat, qry, ct, w_in_t, gain, w_qkv_t, w_qkv, w_out_t, w_out, w_head)


def unpack_kernel(x_ref, g_in, g_gain, g_qkv, g_out, g_head):
    for j in range(9):
        g_qkv[:, j * 128 : j * 128 + 128] = x_ref[j * 384 : j * 384 + 384, :].astype(F32)
    for j in range(3):
        lanes = slice(j * 128, j * 128 + 128)
        g_out[:, lanes] = x_ref[3456 + j * 384 : 3840 + j * 384, :].astype(F32)
        g_in[:, lanes] = x_ref[4608 + j * 128 : 4736 + j * 128, :].astype(F32)
        tail = x_ref[4992 + j * 16 : 5008 + j * 16, :].astype(F32)
        g_head[:, lanes] = tail[:4]
        g_gain[:, lanes] = tail[4:5]


def unpack(x):
    vm = pl.BlockSpec(memory_space=pltpu.VMEM)
    g_in, g_gain, g_qkv, g_out, g_head = pl.pallas_call(
        unpack_kernel,
        out_shape=(
            jax.ShapeDtypeStruct((128, HID), F32),
            jax.ShapeDtypeStruct((1, HID), F32),
            jax.ShapeDtypeStruct((HID, 3 * HID), F32),
            jax.ShapeDtypeStruct((HID, HID), F32),
            jax.ShapeDtypeStruct((4, HID), F32),
        ),
        in_specs=[vm],
        out_specs=(vm,) * 5,
        name="unpack",
    )(x)
    return g_in, g_gain.reshape(HID), g_qkv, g_out, g_head


def swap(x, axis):
    return lax.all_to_all(x, axis, split_axis=0, concat_axis=0, tiled=True)


def fold(x, n):
    return jnp.sum(x.reshape(n, x.shape[0] // n, x.shape[1]).astype(F32), axis=0).astype(BF16)


def sum_all(x):
    x = fold(swap(x, "frame"), 8)
    x = fold(swap(x, "dp"), 32)
    x = swap(jnp.tile(x, (32, 1)), "dp")
    return swap(jnp.tile(x, (8, 1)), "frame")


def body(
    features,
    vis_block,
    vis_count,
    query_frame,
    query_block,
    query_cell,
    cotangent,
    w_in,
    gain,
    w_qkv,
    w_out,
    w_head,
):
    feats = features[0]
    fr_dev = feats.shape[0]
    frame_pos = lax.axis_index("frame")
    local = query_frame[0] - frame_pos * fr_dev
    inside = (local >= 0) & (local < fr_dev)
    picked = feats[jnp.clip(local, 0, fr_dev - 1), query_block[0], query_cell[0]]
    picked = jnp.where(inside[:, None], picked, jnp.zeros((), BF16))
    queries = swap(picked, "frame").reshape(8, 32, 128)
    frame_ids = jnp.arange(fr_dev, dtype=jnp.int32)[None, :, None]
    patches = feats[frame_ids, vis_block[0]]
    live = jnp.arange(2, dtype=jnp.int32)[None, None, :] < vis_count[0][:, :, None]
    patches = jnp.where(live[..., None, None], patches, jnp.zeros((), BF16))
    arrived = swap(patches.reshape(16 * 256, 128), "frame").reshape(8, 512, 128)
    ct = cotangent[0].reshape(4, 4, 8, 16).transpose(0, 1, 3, 2).reshape(4, TOK)
    ct = jnp.pad(ct, ((0, 12), (0, 0)))
    packed = token_grads(
        arrived,
        queries,
        ct,
        w_in.T,
        jnp.broadcast_to(gain[:, None], (HID, 128)),
        w_qkv.T,
        w_qkv,
        w_out.T,
        w_out,
        jnp.pad(w_head, ((0, 12), (0, 0))),
    )
    return unpack(sum_all(packed))


def solution(mesh):
    in_specs = (
        P("dp", "frame", None, None, None),
        P("dp", None, "frame", None),
        P("dp", None, "frame"),
        P("dp", None),
        P("dp", None),
        P("dp", None),
        P("dp", None, "frame", None),
        P(),
        P(),
        P(),
        P(),
        P(),
    )
    out_specs = (P(), P(), P(), P(), P())
    return jax.shard_map(body, mesh=mesh, in_specs=in_specs, out_specs=out_specs, check_vma=False)
```

```python
import jax
import jax.numpy as jnp
from jax import lax
from jax.experimental import pallas as pl
from jax.experimental.pallas import tpu as pltpu
from jax.sharding import PartitionSpec as P

HEADS = 8
SIZE = 48
HID = 384
TOK = 512
HALF = 2560
F32 = jnp.float32
BF16 = jnp.bfloat16


def dot(left, right, dims=((1,), (0,))):
    return lax.dot_general(left, right, (dims, ((), ())), preferred_element_type=F32)


NT = ((1,), (1,))
TN = ((0,), (0,))


def gather_kernel(vis_ref, count_ref, qf_ref, qb_ref, qc_ref, feats_ref, out_ref):
    base = lax.axis_index("frame") * 2
    for g in range(16):
        for fr in range(2):
            shown = count_ref[0, g, fr]
            for k in range(2):
                at = (g // 2, pl.ds(((g % 2) * 2 + fr) * 128 + k * 64, 64))
                tile = feats_ref[0, fr, vis_ref[0, g, fr, k]]
                if k:
                    tile = jnp.where(shown > k, tile, jnp.zeros_like(tile))
                out_ref[at] = tile
    local = qf_ref[...] - base
    index = local * 2048 + qb_ref[...] * 64 + qc_ref[...]
    index = jnp.where((local >= 0) & (local < 2), index, -1)
    column = jnp.broadcast_to(index, (128, 256)).T[:, :1]
    query = jnp.zeros((256, 128), F32)
    for j in range(8):
        lanes = lax.broadcasted_iota(jnp.int32, (256, 512), 1) + j * 512
        chosen = jnp.where(lanes == column, 1.0, 0.0).astype(BF16)
        rows = feats_ref[0, j // 4, (j % 4) * 8 : (j % 4) * 8 + 8].reshape(512, 128)
        query = query + dot(chosen, rows)
    out_ref[:, 512:544, :] = query.astype(BF16).reshape(8, 32, 128)


def gather(vis_block, vis_count, query_frame, query_block, query_cell, features):
    vm = pl.BlockSpec(memory_space=pltpu.VMEM)
    sm = pl.BlockSpec(memory_space=pltpu.SMEM)
    return pl.pallas_call(
        gather_kernel,
        out_shape=jax.ShapeDtypeStruct((8, 544, 128), BF16),
        in_specs=[sm, sm, vm, vm, vm, vm],
        out_specs=vm,
        name="gather",
    )(vis_block, vis_count, query_frame, query_block, query_cell, features)


def token_kernel(
    pat_ref,
    ct_ref,
    w_in_t,
    gain_in,
    w_qkv_t,
    w_qkv,
    w_out_t,
    w_out,
    w_head,
    keep_ref,
    send_ref,
    corr32,
    corr16,
    x_zero,
    normed,
    left,
    qkv,
    d_y,
    d_mixed,
    right,
    inv_ref,
    g_in_ref,
    gain_ref,
):
    hidden, mixed = left.at[0], left.at[1]
    d_qkv, d_y16 = right.at[0:1152], right.at[1152:1536]
    core = lax.axis_index("frame") % 2
    gain_ref[...] = jnp.broadcast_to(gain_in[...], (128, HID)).T
    query = jnp.sum(pat_ref[:, 512:544, :].astype(F32), axis=0).astype(BF16)
    scale = 128 ** (-0.5)
    for g in range(2):
        for s in range(8):
            part = dot(query[g * 16 : g * 16 + 16], pat_ref[s, g * 256 : g * 256 + 256], NT) * scale
            for half in range(2):
                for fr in range(2):
                    row = (g * 2 + half) * 128 + (s * 2 + fr) * 8
                    corr32[row : row + 8, :] = part[half * 8 : half * 8 + 8, fr * 128 : fr * 128 + 128]
    corr16[...] = corr32[...].astype(BF16)

    ct = ct_ref[...]
    for c in range(2):
        cols = slice(c * 256, c * 256 + 256)
        x0 = dot(w_in_t[...], corr16[cols, :], NT)
        x_zero[:, cols] = x0
        mean = jnp.mean(x0, axis=0, keepdims=True)
        centred = x0 - mean
        inv = lax.rsqrt(jnp.mean(centred * centred, axis=0, keepdims=True) + 1e-05)
        nrm = centred * inv
        inv_ref[:, cols] = jnp.broadcast_to(inv, (8, 256))
        normed[:, cols] = nrm
        hid = (nrm * gain_ref[:, :1]).astype(BF16)
        hidden[:, cols] = hid
        for r in range(3):
            rows = slice(r * 384, r * 384 + 384)
            qkv[rows, cols] = dot(w_qkv_t[rows, :], hid).astype(BF16)
        dy = dot(w_head[...], ct[:, cols], TN)
        d_y[:, cols] = dy
        dy16 = dy.astype(BF16)
        d_y16[:, cols] = dy16
        d_mixed[:, cols] = dot(w_out[...], dy16).astype(BF16)

    own = (
        lax.broadcasted_iota(jnp.int32, (8, 128), 0)
        == lax.broadcasted_iota(jnp.int32, (8, 128), 1) % 8
    ).astype(F32)
    a_scale = SIZE ** (-0.5)

    def block(b, carry):
        cols = pl.ds(pl.multiple_of(b * 128, 128), 128)
        for h in range(HEADS):
            rq = slice(h * SIZE, h * SIZE + SIZE)
            rk = slice(HID + h * SIZE, HID + h * SIZE + SIZE)
            rv = slice(2 * HID + h * SIZE, 2 * HID + h * SIZE + SIZE)
            q_t, k_t, v_t = qkv[rq, cols], qkv[rk, cols], qkv[rv, cols]
            d_a = d_mixed[rq, cols]
            score = dot(k_t, q_t, TN).reshape(16, 8, 128) * a_scale
            expo = jnp.exp(score - jnp.max(score, axis=0, keepdims=True))
            prob = expo * (own / jnp.sum(expo, axis=0))[None]
            prob16 = prob.reshape(128, 128).astype(BF16)
            mixed[rq, cols] = dot(v_t, prob16).astype(BF16)
            d_p = dot(v_t, d_a, TN).astype(BF16).astype(F32).reshape(16, 8, 128)
            inner = jnp.sum(d_p * prob, axis=0, keepdims=True)
            d_s = (prob * (d_p - inner) * a_scale).reshape(128, 128).astype(BF16)
            d_qkv[rq, cols] = dot(k_t, d_s).astype(BF16)
            d_qkv[rk, cols] = dot(q_t, d_s, NT).astype(BF16)
            d_qkv[rv, cols] = dot(d_a, prob16, NT).astype(BF16)
        return carry

    lax.fori_loop(0, 4, block, 0)

    head = jnp.zeros((16, HID), F32)
    gain_sum = jnp.zeros((HID, 128), F32)
    g_in = jnp.zeros((128, HID), F32)
    for c in range(2):
        cols = slice(c * 256, c * 256 + 256)
        y16 = (x_zero[:, cols] + dot(w_out_t[...], mixed[:, cols])).astype(BF16)
        head = head + dot(ct[:, cols], y16, NT)
        dh = dot(w_qkv[...], d_qkv[:, cols])
        nrm = normed[:, cols]
        prod = dh * nrm
        gain_sum = gain_sum + prod[:, :128] + prod[:, 128:]
        gain = gain_ref[:, :1]
        dn = dh * gain
        m_one = jnp.mean(dn, axis=0, keepdims=True)
        m_two = jnp.mean(dn * nrm, axis=0, keepdims=True)
        dx = inv_ref[:1, cols] * (dn - m_one - nrm * m_two) + d_y[:, cols]
        g_in = g_in + dot(corr16[cols, :], dx.astype(BF16), ((0,), (1,)))
    gain_row = jnp.sum(gain_sum.T, axis=0, keepdims=True)
    at_four = lax.broadcasted_iota(jnp.int32, (16, HID), 0) == 4
    head = jnp.where(at_four, jnp.broadcast_to(gain_row, (16, HID)), head)
    for j in range(3):
        g_in_ref[j * 128 : j * 128 + 128, :] = g_in[:, j * 128 : j * 128 + 128]
    for ref, half in ((keep_ref, core), (send_ref, 1 - core)):
        for i in range(2):
            j = half * 2 + i
            rows = pl.ds(pl.multiple_of(j * HID, HID), HID)
            part = dot(left[jnp.where(j == 3, 1, 0)], right[rows, :], NT)
            for n in range(3):
                at = (i * 3 + n) * HID
                ref[at : at + HID, :] = part[:, n * 128 : n * 128 + 128].astype(BF16)
        ref[2304:2496, :] = g_in_ref[pl.ds(pl.multiple_of(half * 192, 8), 192), :].astype(BF16)
        part = jnp.where(half == 0, head, 0.0).astype(BF16)
        for n in range(3):
            ref[2496 + n * 16 : 2512 + n * 16, :] = part[:, n * 128 : n * 128 + 128]
        ref[2544:HALF, :] = jnp.zeros((HALF - 2544, 128), BF16)


def token_grads(pat, ct, w_in_t, gain, w_qkv_t, w_qkv, w_out_t, w_out, w_head):
    vm = pl.BlockSpec(memory_space=pltpu.VMEM)
    half = jax.ShapeDtypeStruct((HALF, 128), BF16)
    return pl.pallas_call(
        token_kernel,
        out_shape=(half, half),
        in_specs=[vm] * 9,
        out_specs=(vm, vm),
        scratch_shapes=[
            pltpu.VMEM((TOK, 128), F32),
            pltpu.VMEM((TOK, 128), BF16),
            pltpu.VMEM((HID, TOK), F32),
            pltpu.VMEM((HID, TOK), F32),
            pltpu.VMEM((2, HID, TOK), BF16),
            pltpu.VMEM((3 * HID, TOK), BF16),
            pltpu.VMEM((HID, TOK), F32),
            pltpu.VMEM((HID, TOK), BF16),
            pltpu.VMEM((4 * HID, TOK), BF16),
            pltpu.VMEM((8, TOK), F32),
            pltpu.VMEM((HID, 128), F32),
            pltpu.VMEM((HID, 128), F32),
        ],
        name="token_grads",
    )(pat, ct, w_in_t, gain, w_qkv_t, w_qkv, w_out_t, w_out, w_head)


def unpack_kernel(own_ref, other_ref, g_in, g_gain, g_qkv, g_out, g_head):
    core = lax.axis_index("frame") % 2

    def write(low, high):
        for j in range(3):
            lanes = slice(j * 128, j * 128 + 128)
            first, second = slice(j * HID, j * HID + HID), slice((j + 3) * HID, (j + 4) * HID)
            g_qkv[:, lanes] = low[first, :].astype(F32)
            g_qkv[:, HID + j * 128 : HID + j * 128 + 128] = low[second, :].astype(F32)
            g_qkv[:, 2 * HID + j * 128 : 2 * HID + j * 128 + 128] = high[first, :].astype(F32)
            g_out[:, lanes] = high[second, :].astype(F32)
            tail = low[2496 + j * 16 : 2512 + j * 16, :].astype(F32)
            g_head[:, lanes] = tail[:4]
            g_gain[lanes] = tail[4]
        g_in[:, 0:128] = low[2304:2432, :].astype(F32)
        g_in[0:64, 128:256] = low[2432:2496, :].astype(F32)
        g_in[64:128, 128:256] = high[2304:2368, :].astype(F32)
        g_in[:, 256:384] = high[2368:2496, :].astype(F32)

    @pl.when(core == 0)
    def _():
        write(own_ref, other_ref)

    @pl.when(core == 1)
    def _():
        write(other_ref, own_ref)


def unpack(own, other):
    vm = pl.BlockSpec(memory_space=pltpu.VMEM)
    return pl.pallas_call(
        unpack_kernel,
        out_shape=(
            jax.ShapeDtypeStruct((128, HID), F32),
            jax.ShapeDtypeStruct((HID,), F32),
            jax.ShapeDtypeStruct((HID, 3 * HID), F32),
            jax.ShapeDtypeStruct((HID, HID), F32),
            jax.ShapeDtypeStruct((4, HID), F32),
        ),
        in_specs=[vm, vm],
        out_specs=(vm,) * 5,
        name="unpack",
    )(own, other)


Y_GROUPS = [[0, 2, 4, 6], [1, 3, 5, 7]]
PARTNER = [(i, i ^ 1) for i in range(8)]


def swap(x, axis, groups=None):
    return lax.all_to_all(
        x, axis, split_axis=0, concat_axis=0, axis_index_groups=groups, tiled=True
    )


def fold(x, n):
    return jnp.sum(x.reshape(n, x.shape[0] // n, x.shape[1]).astype(F32), axis=0).astype(BF16)


def sum_all(keep, send):
    x = (keep.astype(F32) + lax.ppermute(send, "frame", PARTNER).astype(F32)).astype(BF16)
    x = fold(swap(x, "frame", Y_GROUPS), 4)
    x = fold(swap(x, "dp"), 32)
    x = swap(jnp.tile(x, (32, 1)), "dp")
    x = swap(jnp.tile(x, (4, 1)), "frame", Y_GROUPS)
    return x, lax.ppermute(x, "frame", PARTNER)


def body(
    features,
    vis_block,
    vis_count,
    query_frame,
    query_block,
    query_cell,
    cotangent,
    w_in,
    gain,
    w_qkv,
    w_out,
    w_head,
):
    outgoing = gather(vis_block, vis_count, query_frame, query_block, query_cell, features)
    arrived = swap(outgoing, "frame")
    ct = cotangent[0].reshape(4, 4, 8, 16).transpose(0, 1, 3, 2).reshape(4, TOK)
    ct = jnp.pad(ct, ((0, 12), (0, 0)))
    keep, send = token_grads(
        arrived,
        ct,
        w_in.T,
        gain.reshape(1, HID),
        w_qkv.T,
        w_qkv,
        w_out.T,
        w_out,
        jnp.pad(w_head, ((0, 12), (0, 0))),
    )
    return unpack(*sum_all(keep, send))


def solution(mesh):
    in_specs = (
        P("dp", "frame", None, None, None),
        P("dp", None, "frame", None),
        P("dp", None, "frame"),
        P("dp", None),
        P("dp", None),
        P("dp", None),
        P("dp", None, "frame", None),
        P(),
        P(),
        P(),
        P(),
        P(),
    )
    out_specs = (P(), P(), P(), P(), P())
    return jax.shard_map(body, mesh=mesh, in_specs=in_specs, out_specs=out_specs, check_vma=False)
```

```python
import jax
import jax.numpy as jnp
from jax import lax
from jax.experimental import pallas as pl
from jax.experimental.pallas import tpu as pltpu
from jax.sharding import PartitionSpec as P

HEADS = 8
SIZE = 48
HID = 384
TOK = 512
HALF = 2560
F32 = jnp.float32
BF16 = jnp.bfloat16


def dot(left, right, dims=((1,), (0,))):
    return lax.dot_general(left, right, (dims, ((), ())), preferred_element_type=F32)


NT = ((1,), (1,))
TN = ((0,), (0,))


def gather_kernel(vis_ref, count_ref, qf_ref, qb_ref, qc_ref, feats_ref, out_ref):
    base = lax.axis_index("frame") * 2
    for g in range(16):
        for fr in range(2):
            shown = count_ref[0, fr, g]
            for k in range(2):
                at = (g // 2, pl.ds(((g % 2) * 2 + fr) * 128 + k * 64, 64))
                tile = feats_ref[0, fr, vis_ref[0, fr, k, g]]
                if k:
                    tile = jnp.where(shown > k, tile, jnp.zeros_like(tile))
                out_ref[at] = tile
    local = qf_ref[...] - base
    index = local * 2048 + qb_ref[...] * 64 + qc_ref[...]
    index = jnp.where((local >= 0) & (local < 2), index, -1)
    column = jnp.broadcast_to(index, (128, 256)).T[:, :1]
    query = jnp.zeros((256, 128), F32)
    for j in range(8):
        lanes = lax.broadcasted_iota(jnp.int32, (256, 512), 1) + j * 512
        chosen = jnp.where(lanes == column, 1.0, 0.0).astype(BF16)
        rows = feats_ref[0, j // 4, (j % 4) * 8 : (j % 4) * 8 + 8].reshape(512, 128)
        query = query + dot(chosen, rows)
    out_ref[:, 512:544, :] = query.astype(BF16).reshape(8, 32, 128)


def gather(vis_block, vis_count, query_frame, query_block, query_cell, features):
    vm = pl.BlockSpec(memory_space=pltpu.VMEM)
    sm = pl.BlockSpec(memory_space=pltpu.SMEM)
    return pl.pallas_call(
        gather_kernel,
        out_shape=jax.ShapeDtypeStruct((8, 544, 128), BF16),
        in_specs=[sm, sm, vm, vm, vm, vm],
        out_specs=vm,
        name="gather",
    )(vis_block.transpose(0, 2, 3, 1), vis_count.transpose(0, 2, 1), query_frame, query_block, query_cell, features)


def token_kernel(
    pat_ref,
    ct_ref,
    w_in,
    gain_in,
    w_qkv_t,
    w_qkv,
    w_out_t,
    w_out,
    w_head,
    keep_ref,
    send_ref,
    corr32,
    corr16,
    x_zero,
    normed,
    left,
    qkv,
    d_y,
    d_mixed,
    right,
    inv_ref,
    g_in_ref,
    gain_ref,
    s_ref,
    t_ref,
    p_ref,
    d_ref,
):
    hidden, mixed = left.at[0], left.at[1]
    d_qkv, d_y16 = right.at[0:1152], right.at[1152:1536]
    core = lax.axis_index("frame") % 2
    gain_ref[...] = jnp.broadcast_to(gain_in[...], (128, HID)).T
    query = jnp.sum(pat_ref[:, 512:544, :].astype(F32), axis=0).astype(BF16)
    scale = 128 ** (-0.5)
    for g in range(2):
        for s in range(8):
            part = dot(query[g * 16 : g * 16 + 16], pat_ref[s, g * 256 : g * 256 + 256], NT) * scale
            for half in range(2):
                for fr in range(2):
                    row = (g * 2 + half) * 128 + (s * 2 + fr) * 8
                    corr32[row : row + 8, :] = part[half * 8 : half * 8 + 8, fr * 128 : fr * 128 + 128]
    corr16[...] = corr32[...].astype(BF16)

    ct = ct_ref[...]
    gain = gain_ref[...]
    for c in range(2):
        wide = slice(c * 256, c * 256 + 256)
        dy = dot(w_head[...], ct[:, wide], TN)
        d_y[:, wide] = dy
        d_y16[:, wide] = dy.astype(BF16)
        d_mixed[:, wide] = dot(w_out[...], d_y16[:, wide]).astype(BF16)
        x_zero[:, wide] = dot(w_in[...], corr16[wide, :], ((0,), (1,)))
        for n in range(2):
            cols = slice(c * 256 + n * 128, c * 256 + n * 128 + 128)
            x0 = x_zero[:, cols]
            centred = x0 - jnp.mean(x0, axis=0, keepdims=True)
            inv = lax.rsqrt(jnp.mean(centred * centred, axis=0, keepdims=True) + 1e-05)
            inv_ref[:, cols] = jnp.broadcast_to(inv, (8, 128))
            nrm = centred * inv
            normed[:, cols] = nrm
            hidden[:, cols] = (nrm * gain).astype(BF16)
        for r in range(3):
            rows = slice(r * 384, r * 384 + 384)
            qkv[rows, wide] = dot(w_qkv_t[rows, :], hidden[:, wide]).astype(BF16)

    own = (
        lax.broadcasted_iota(jnp.int32, (8, 128), 0)
        == lax.broadcasted_iota(jnp.int32, (8, 128), 1) % 8
    ).astype(F32)
    a_scale = SIZE ** (-0.5)
    e_scale = a_scale * 1.4426950408889634

    def block(b, carry):
        def cols(h):
            return pl.ds(pl.multiple_of((b * 2 + h // HEADS) * 128, 128), 128)

        def rows(h, n):
            at = n * HID + h % HEADS * SIZE
            return slice(at, at + SIZE)

        def scores(h):
            s_ref[h] = dot(qkv[rows(h, 1), cols(h)], qkv[rows(h, 0), cols(h)], TN)
            t_ref[h] = dot(qkv[rows(h, 2), cols(h)], d_mixed[rows(h, 0), cols(h)], TN).astype(BF16)

        def weights(h):
            score = s_ref[h].reshape(16, 8, 128)
            expo = jnp.exp2((score - jnp.max(score, axis=0, keepdims=True)) * e_scale)
            prob = expo * (own / jnp.sum(expo, axis=0))[None]
            p_ref[h] = prob.reshape(128, 128).astype(BF16)
            d_p = t_ref[h].astype(F32).reshape(16, 8, 128)
            inner = jnp.sum(d_p * prob, axis=0, keepdims=True)
            d_ref[h] = (prob * (d_p - inner)).reshape(128, 128).astype(BF16)

        def products(h):
            prob, d_s = p_ref[h], d_ref[h]
            mixed[rows(h, 0), cols(h)] = dot(qkv[rows(h, 2), cols(h)], prob).astype(BF16)
            d_v = dot(d_mixed[rows(h, 0), cols(h)], prob, NT)
            d_q = dot(qkv[rows(h, 1), cols(h)], d_s) * a_scale
            d_k = dot(qkv[rows(h, 0), cols(h)], d_s, NT) * a_scale
            d_qkv[rows(h, 0), cols(h)] = d_q.astype(BF16)
            d_qkv[rows(h, 1), cols(h)] = d_k.astype(BF16)
            d_qkv[rows(h, 2), cols(h)] = d_v.astype(BF16)

        for h in range(2 * HEADS + 2):
            if h < 2 * HEADS:
                scores(h)
            if 1 <= h <= 2 * HEADS:
                weights(h - 1)
            if h >= 2:
                products(h - 2)
        return carry

    lax.fori_loop(0, 2, block, 0)

    def pair_grads(ref, half, i):
        j = half * 2 + i
        rows = pl.ds(pl.multiple_of(j * HID, HID), HID)
        part = dot(left[jnp.where(j == 3, 1, 0)], right[rows, :], NT)
        for n in range(3):
            at = (i * 3 + n) * HID
            ref[at : at + HID, :] = part[:, n * 128 : n * 128 + 128].astype(BF16)

    head = jnp.zeros((16, HID), F32)
    gain_sum = jnp.zeros((HID, 128), F32)
    for c in range(2):
        wide = slice(c * 256, c * 256 + 256)
        y16 = (x_zero[:, wide] + dot(w_out_t[...], mixed[:, wide])).astype(BF16)
        head = head + dot(ct[:, wide], y16, NT)
        x_zero[:, wide] = dot(w_qkv[...], d_qkv[:, wide])
        for n in range(2):
            cols = slice(c * 256 + n * 128, c * 256 + n * 128 + 128)
            pair_grads(*((send_ref, 1 - core, n), (keep_ref, core, n))[c])
            dh, nrm = x_zero[:, cols], normed[:, cols]
            gain_sum = gain_sum + dh * nrm
            dn = dh * gain
            m_one = jnp.mean(dn, axis=0, keepdims=True)
            m_two = jnp.mean(dn * nrm, axis=0, keepdims=True)
            dx = inv_ref[:1, cols] * (dn - m_one - nrm * m_two) + d_y[:, cols]
            d_mixed[:, cols] = dx.astype(BF16)
    g_in = dot(corr16[...], d_mixed[...], ((0,), (1,)))
    gain_row = jnp.sum(gain_sum.T, axis=0, keepdims=True)
    at_four = lax.broadcasted_iota(jnp.int32, (16, HID), 0) == 4
    head = jnp.where(at_four, jnp.broadcast_to(gain_row, (16, HID)), head)
    for j in range(3):
        g_in_ref[j * 128 : j * 128 + 128, :] = g_in[:, j * 128 : j * 128 + 128]
    for ref, half in ((keep_ref, core), (send_ref, 1 - core)):
        ref[2304:2496, :] = g_in_ref[pl.ds(pl.multiple_of(half * 192, 8), 192), :].astype(BF16)
        part = jnp.where(half == 0, head, 0.0).astype(BF16)
        for n in range(3):
            ref[2496 + n * 16 : 2512 + n * 16, :] = part[:, n * 128 : n * 128 + 128]
        ref[2544:HALF, :] = jnp.zeros((HALF - 2544, 128), BF16)


def token_grads(pat, ct, w_in, gain, w_qkv_t, w_qkv, w_out_t, w_out, w_head):
    vm = pl.BlockSpec(memory_space=pltpu.VMEM)
    half = jax.ShapeDtypeStruct((HALF, 128), BF16)
    return pl.pallas_call(
        token_kernel,
        out_shape=(half, half),
        in_specs=[vm] * 9,
        out_specs=(vm, vm),
        scratch_shapes=[
            pltpu.VMEM((TOK, 128), F32),
            pltpu.VMEM((TOK, 128), BF16),
            pltpu.VMEM((HID, TOK), F32),
            pltpu.VMEM((HID, TOK), F32),
            pltpu.VMEM((2, HID, TOK), BF16),
            pltpu.VMEM((3 * HID, TOK), BF16),
            pltpu.VMEM((HID, TOK), F32),
            pltpu.VMEM((HID, TOK), BF16),
            pltpu.VMEM((4 * HID, TOK), BF16),
            pltpu.VMEM((8, TOK), F32),
            pltpu.VMEM((HID, 128), F32),
            pltpu.VMEM((HID, 128), F32),
            pltpu.VMEM((2 * HEADS, 128, 128), F32),
            pltpu.VMEM((2 * HEADS, 128, 128), BF16),
            pltpu.VMEM((2 * HEADS, 128, 128), BF16),
            pltpu.VMEM((2 * HEADS, 128, 128), BF16),
        ],
        compiler_params=pltpu.CompilerParams(vmem_limit_bytes=28 << 20),
        name="token_grads",
    )(pat, ct, w_in, gain, w_qkv_t, w_qkv, w_out_t, w_out, w_head)


def unpack_kernel(own_ref, other_ref, g_in, g_gain, g_qkv, g_out, g_head):
    core = lax.axis_index("frame") % 2

    def write(low, high):
        for j in range(3):
            lanes = slice(j * 128, j * 128 + 128)
            first, second = slice(j * HID, j * HID + HID), slice((j + 3) * HID, (j + 4) * HID)
            g_qkv[:, lanes] = low[first, :].astype(F32)
            g_qkv[:, HID + j * 128 : HID + j * 128 + 128] = low[second, :].astype(F32)
            g_qkv[:, 2 * HID + j * 128 : 2 * HID + j * 128 + 128] = high[first, :].astype(F32)
            g_out[:, lanes] = high[second, :].astype(F32)
            tail = low[2496 + j * 16 : 2512 + j * 16, :].astype(F32)
            g_head[:, lanes] = tail[:4]
            g_gain[lanes] = tail[4]
        g_in[:, 0:128] = low[2304:2432, :].astype(F32)
        g_in[0:64, 128:256] = low[2432:2496, :].astype(F32)
        g_in[64:128, 128:256] = high[2304:2368, :].astype(F32)
        g_in[:, 256:384] = high[2368:2496, :].astype(F32)

    @pl.when(core == 0)
    def _():
        write(own_ref, other_ref)

    @pl.when(core == 1)
    def _():
        write(other_ref, own_ref)


def unpack(own, other):
    vm = pl.BlockSpec(memory_space=pltpu.VMEM)
    return pl.pallas_call(
        unpack_kernel,
        out_shape=(
            jax.ShapeDtypeStruct((128, HID), F32),
            jax.ShapeDtypeStruct((HID,), F32),
            jax.ShapeDtypeStruct((HID, 3 * HID), F32),
            jax.ShapeDtypeStruct((HID, HID), F32),
            jax.ShapeDtypeStruct((4, HID), F32),
        ),
        in_specs=[vm, vm],
        out_specs=(vm,) * 5,
        compiler_params=pltpu.CompilerParams(vmem_limit_bytes=12 << 20),
        name="unpack",
    )(own, other)


Y_GROUPS = [[0, 2, 4, 6], [1, 3, 5, 7]]
PARTNER = [(i, i ^ 1) for i in range(8)]


def swap(x, axis, groups=None):
    return lax.all_to_all(
        x, axis, split_axis=0, concat_axis=0, axis_index_groups=groups, tiled=True
    )


def fold(x, n):
    return jnp.sum(x.reshape(n, x.shape[0] // n, x.shape[1]).astype(F32), axis=0).astype(BF16)


def sum_all(keep, send):
    x = (keep.astype(F32) + lax.ppermute(send, "frame", PARTNER).astype(F32)).astype(BF16)
    x = fold(swap(x, "frame", Y_GROUPS), 4)
    x = fold(swap(x, "dp"), 32)
    x = swap(jnp.tile(x, (32, 1)), "dp")
    x = swap(jnp.tile(x, (4, 1)), "frame", Y_GROUPS)
    return x, lax.ppermute(x, "frame", PARTNER)


def body(
    features,
    vis_block,
    vis_count,
    query_frame,
    query_block,
    query_cell,
    cotangent,
    w_in,
    gain,
    w_qkv,
    w_out,
    w_head,
):
    outgoing = gather(vis_block, vis_count, query_frame, query_block, query_cell, features)
    arrived = swap(outgoing, "frame")
    ct = cotangent[0].reshape(4, 4, 8, 16).transpose(0, 1, 3, 2).reshape(4, TOK)
    ct = jnp.pad(ct, ((0, 12), (0, 0)))
    keep, send = token_grads(
        arrived,
        ct,
        w_in,
        gain.reshape(1, HID),
        w_qkv.T,
        w_qkv,
        w_out.T,
        w_out,
        jnp.pad(w_head, ((0, 12), (0, 0))),
    )
    return unpack(*sum_all(keep, send))


def solution(mesh):
    in_specs = (
        P("dp", "frame", None, None, None),
        P("dp", None, "frame", None),
        P("dp", None, "frame"),
        P("dp", None),
        P("dp", None),
        P("dp", None),
        P("dp", None, "frame", None),
        P(),
        P(),
        P(),
        P(),
        P(),
    )
    out_specs = (P(), P(), P(), P(), P())
    return jax.shard_map(body, mesh=mesh, in_specs=in_specs, out_specs=out_specs, check_vma=False)
```

```python
import functools

import jax
import jax.numpy as jnp
from jax import lax
from jax.experimental import pallas as pl
from jax.experimental.pallas import tpu as pltpu
from jax.sharding import PartitionSpec as P

HEADS = 8
SIZE = 48
HID = 384
TOK = 512
HALF = 2560
F32 = jnp.float32
BF16 = jnp.bfloat16


def dot(left, right, dims=((1,), (0,))):
    return lax.dot_general(left, right, (dims, ((), ())), preferred_element_type=F32)


NT = ((1,), (1,))
TN = ((0,), (0,))


def gather_kernel(vis_ref, count_ref, qf_ref, qb_ref, qc_ref, feats_ref, out_ref):
    base = lax.axis_index("frame") * 2
    for g in range(16):
        for fr in range(2):
            shown = count_ref[0, fr, g]
            for k in range(2):
                at = (g // 2, pl.ds(((g % 2) * 2 + fr) * 128 + k * 64, 64))
                tile = feats_ref[0, fr, vis_ref[0, fr, k, g]]
                if k:
                    tile = jnp.where(shown > k, tile, jnp.zeros_like(tile))
                out_ref[at] = tile
    local = qf_ref[...] - base
    index = local * 2048 + qb_ref[...] * 64 + qc_ref[...]
    index = jnp.where((local >= 0) & (local < 2), index, -1)
    column = jnp.broadcast_to(index, (128, 256)).T[:, :1]
    query = jnp.zeros((256, 128), F32)
    for j in range(8):
        lanes = lax.broadcasted_iota(jnp.int32, (256, 512), 1) + j * 512
        chosen = jnp.where(lanes == column, 1.0, 0.0).astype(BF16)
        rows = feats_ref[0, j // 4, (j % 4) * 8 : (j % 4) * 8 + 8].reshape(512, 128)
        query = query + dot(chosen, rows)
    out_ref[:, 512:544, :] = query.astype(BF16).reshape(8, 32, 128)


def gather(vis_block, vis_count, query_frame, query_block, query_cell, features):
    vm = pl.BlockSpec(memory_space=pltpu.VMEM)
    sm = pl.BlockSpec(memory_space=pltpu.SMEM)
    return pl.pallas_call(
        gather_kernel,
        out_shape=jax.ShapeDtypeStruct((8, 544, 128), BF16),
        in_specs=[sm, sm, vm, vm, vm, vm],
        out_specs=vm,
        name="gather",
    )(vis_block.transpose(0, 2, 3, 1), vis_count.transpose(0, 2, 1), query_frame, query_block, query_cell, features)


def token_kernel(
    pat_ref,
    ct_ref,
    w_ends,
    gain_in,
    w_qkv_t,
    w_qkv,
    w_out,
    keep_ref,
    send_ref,
    corr32,
    corr16,
    x_zero,
    normed,
    left,
    qkv,
    d_y,
    d_mixed,
    right,
    inv_ref,
    g_in_ref,
    gain_ref,
    s_ref,
    t_ref,
    p_ref,
    d_ref,
):
    hidden, mixed = left.at[0], left.at[1]
    d_qkv, d_y16 = right.at[0:1152], right.at[1152:1536]
    core = lax.axis_index("frame") % 2
    gain_ref[...] = jnp.broadcast_to(gain_in[...], (128, HID)).T
    query = jnp.sum(pat_ref[:, 512:544, :].astype(F32), axis=0).astype(BF16)
    scale = 128 ** (-0.5)
    for g in range(2):
        for s in range(8):
            part = dot(query[g * 16 : g * 16 + 16], pat_ref[s, g * 256 : g * 256 + 256], NT) * scale
            for half in range(2):
                for fr in range(2):
                    row = (g * 2 + half) * 128 + (s * 2 + fr) * 8
                    corr32[row : row + 8, :] = part[half * 8 : half * 8 + 8, fr * 128 : fr * 128 + 128]
    corr16[...] = corr32[...].astype(BF16)

    ct = ct_ref[...]
    gain = gain_ref[...]
    for c in range(2):
        wide = slice(c * 256, c * 256 + 256)
        dy = dot(w_ends[128:144, :], ct[:, wide], TN)
        d_y[:, wide] = dy
        d_y16[:, wide] = dy.astype(BF16)
        d_mixed[:, wide] = dot(w_out[...], d_y16[:, wide]).astype(BF16)
        x_zero[:, wide] = dot(w_ends[0:128, :], corr16[wide, :], ((0,), (1,)))
        for n in range(2):
            cols = slice(c * 256 + n * 128, c * 256 + n * 128 + 128)
            x0 = x_zero[:, cols]
            centred = x0 - jnp.mean(x0, axis=0, keepdims=True)
            inv = lax.rsqrt(jnp.mean(centred * centred, axis=0, keepdims=True) + 1e-05)
            inv_ref[:, cols] = jnp.broadcast_to(inv, (8, 128))
            nrm = centred * inv
            normed[:, cols] = nrm
            hidden[:, cols] = (nrm * gain).astype(BF16)
        for r in range(3):
            rows = slice(r * 384, r * 384 + 384)
            qkv[rows, wide] = dot(w_qkv_t[rows, :], hidden[:, wide]).astype(BF16)

    own = (
        lax.broadcasted_iota(jnp.int32, (8, 128), 0)
        == lax.broadcasted_iota(jnp.int32, (8, 128), 1) % 8
    ).astype(F32)
    a_scale = SIZE ** (-0.5)
    e_scale = a_scale * 1.4426950408889634

    def block(b, carry):
        def cols(h):
            return pl.ds(pl.multiple_of((b * 2 + h // HEADS) * 128, 128), 128)

        def rows(h, n):
            at = n * HID + h % HEADS * SIZE
            return slice(at, at + SIZE)

        def scores(h):
            s_ref[h] = dot(qkv[rows(h, 1), cols(h)], qkv[rows(h, 0), cols(h)], TN)
            t_ref[h] = dot(qkv[rows(h, 2), cols(h)], d_mixed[rows(h, 0), cols(h)], TN).astype(BF16)

        def weights(h):
            score = s_ref[h].reshape(16, 8, 128)
            expo = jnp.exp2((score - jnp.max(score, axis=0, keepdims=True)) * e_scale)
            prob = expo * (own / jnp.sum(expo, axis=0))[None]
            p_ref[h] = prob.reshape(128, 128).astype(BF16)
            d_p = t_ref[h].astype(F32).reshape(16, 8, 128)
            inner = jnp.sum(d_p * prob, axis=0, keepdims=True)
            d_ref[h] = (prob * (d_p - inner)).reshape(128, 128).astype(BF16)

        def products(h):
            prob, d_s = p_ref[h], d_ref[h]
            mixed[rows(h, 0), cols(h)] = dot(qkv[rows(h, 2), cols(h)], prob).astype(BF16)
            d_v = dot(d_mixed[rows(h, 0), cols(h)], prob, NT)
            d_q = dot(qkv[rows(h, 1), cols(h)], d_s) * a_scale
            d_k = dot(qkv[rows(h, 0), cols(h)], d_s, NT) * a_scale
            d_qkv[rows(h, 0), cols(h)] = d_q.astype(BF16)
            d_qkv[rows(h, 1), cols(h)] = d_k.astype(BF16)
            d_qkv[rows(h, 2), cols(h)] = d_v.astype(BF16)

        for h in range(2 * HEADS + 2):
            if h < 2 * HEADS:
                scores(h)
            if 1 <= h <= 2 * HEADS:
                weights(h - 1)
            if h >= 2:
                products(h - 2)
        return carry

    lax.fori_loop(0, 2, block, 0)

    def pair_grads(ref, half, i):
        j = half * 2 + i
        rows = pl.ds(pl.multiple_of(j * HID, HID), HID)
        part = dot(left[jnp.where(j == 3, 1, 0)], right[rows, :], NT)
        for n in range(3):
            at = (i * 3 + n) * HID
            ref[at : at + HID, :] = part[:, n * 128 : n * 128 + 128].astype(BF16)

    head = jnp.zeros((16, HID), F32)
    gain_sum = jnp.zeros((HID, 128), F32)
    for c in range(2):
        wide = slice(c * 256, c * 256 + 256)
        y16 = (x_zero[:, wide] + dot(w_out[...], mixed[:, wide], TN)).astype(BF16)
        head = head + dot(ct[:, wide], y16, NT)
        x_zero[:, wide] = dot(w_qkv[...], d_qkv[:, wide])
        for n in range(2):
            cols = slice(c * 256 + n * 128, c * 256 + n * 128 + 128)
            pair_grads(*((send_ref, 1 - core, n), (keep_ref, core, n))[c])
            dh, nrm = x_zero[:, cols], normed[:, cols]
            gain_sum = gain_sum + dh * nrm
            dn = dh * gain
            m_one = jnp.mean(dn, axis=0, keepdims=True)
            m_two = jnp.mean(dn * nrm, axis=0, keepdims=True)
            dx = inv_ref[:1, cols] * (dn - m_one - nrm * m_two) + d_y[:, cols]
            d_mixed[:, cols] = dx.astype(BF16)
    g_in = dot(corr16[...], d_mixed[...], ((0,), (1,)))
    gain_row = jnp.sum(gain_sum.T, axis=0, keepdims=True)
    at_four = lax.broadcasted_iota(jnp.int32, (16, HID), 0) == 4
    head = jnp.where(at_four, jnp.broadcast_to(gain_row, (16, HID)), head)
    for j in range(3):
        g_in_ref[j * 128 : j * 128 + 128, :] = g_in[:, j * 128 : j * 128 + 128]
    for ref, half in ((keep_ref, core), (send_ref, 1 - core)):
        ref[2304:2496, :] = g_in_ref[pl.ds(pl.multiple_of(half * 192, 8), 192), :].astype(BF16)
        part = jnp.where(half == 0, head, 0.0).astype(BF16)
        for n in range(3):
            ref[2496 + n * 16 : 2512 + n * 16, :] = part[:, n * 128 : n * 128 + 128]
        ref[2544:HALF, :] = jnp.zeros((HALF - 2544, 128), BF16)


def token_grads(pat, ct, w_ends, gain, w_qkv_t, w_qkv, w_out):
    vm = pl.BlockSpec(memory_space=pltpu.VMEM)
    half = jax.ShapeDtypeStruct((HALF, 128), BF16)
    return pl.pallas_call(
        token_kernel,
        out_shape=(half, half),
        in_specs=[vm] * 7,
        out_specs=(vm, vm),
        scratch_shapes=[
            pltpu.VMEM((TOK, 128), F32),
            pltpu.VMEM((TOK, 128), BF16),
            pltpu.VMEM((HID, TOK), F32),
            pltpu.VMEM((HID, TOK), F32),
            pltpu.VMEM((2, HID, TOK), BF16),
            pltpu.VMEM((3 * HID, TOK), BF16),
            pltpu.VMEM((HID, TOK), F32),
            pltpu.VMEM((HID, TOK), BF16),
            pltpu.VMEM((4 * HID, TOK), BF16),
            pltpu.VMEM((8, TOK), F32),
            pltpu.VMEM((HID, 128), F32),
            pltpu.VMEM((HID, 128), F32),
            pltpu.VMEM((2 * HEADS, 128, 128), F32),
            pltpu.VMEM((2 * HEADS, 128, 128), BF16),
            pltpu.VMEM((2 * HEADS, 128, 128), BF16),
            pltpu.VMEM((2 * HEADS, 128, 128), BF16),
        ],
        compiler_params=pltpu.CompilerParams(vmem_limit_bytes=28 << 20),
        name="token_grads",
    )(pat, ct, w_ends, gain, w_qkv_t, w_qkv, w_out)


def unpack_kernel(own_ref, other_ref, g_in, g_gain, g_qkv, g_out, g_head):
    core = lax.axis_index("frame") % 2

    def write(low, high):
        for j in range(3):
            lanes = slice(j * 128, j * 128 + 128)
            first, second = slice(j * HID, j * HID + HID), slice((j + 3) * HID, (j + 4) * HID)
            g_qkv[:, lanes] = low[first, :].astype(F32)
            g_qkv[:, HID + j * 128 : HID + j * 128 + 128] = low[second, :].astype(F32)
            g_qkv[:, 2 * HID + j * 128 : 2 * HID + j * 128 + 128] = high[first, :].astype(F32)
            g_out[:, lanes] = high[second, :].astype(F32)
            tail = low[2496 + j * 16 : 2512 + j * 16, :].astype(F32)
            g_head[:, lanes] = tail[:4]
            g_gain[lanes] = tail[4]
        g_in[:, 0:128] = low[2304:2432, :].astype(F32)
        g_in[0:64, 128:256] = low[2432:2496, :].astype(F32)
        g_in[64:128, 128:256] = high[2304:2368, :].astype(F32)
        g_in[:, 256:384] = high[2368:2496, :].astype(F32)

    @pl.when(core == 0)
    def _():
        write(own_ref, other_ref)

    @pl.when(core == 1)
    def _():
        write(other_ref, own_ref)


def unpack(own, other):
    vm = pl.BlockSpec(memory_space=pltpu.VMEM)
    return pl.pallas_call(
        unpack_kernel,
        out_shape=(
            jax.ShapeDtypeStruct((128, HID), F32),
            jax.ShapeDtypeStruct((HID,), F32),
            jax.ShapeDtypeStruct((HID, 3 * HID), F32),
            jax.ShapeDtypeStruct((HID, HID), F32),
            jax.ShapeDtypeStruct((4, HID), F32),
        ),
        in_specs=[vm, vm],
        out_specs=(vm,) * 5,
        compiler_params=pltpu.CompilerParams(vmem_limit_bytes=12 << 20),
        name="unpack",
    )(own, other)


AXES = ("dp", "frame")
PARTNER = [(i, i ^ 1) for i in range(8)]


def make_groups(mesh):
    nx = max(mesh.shape["dp"] // 8, 1)
    nz = mesh.shape["dp"] // nx
    at = lambda x, y, z, c: (x * nz + z) * 8 + y * 2 + c
    plane = [[at(x, y, z, c) for y in range(4) for x in range(nx)] for z in range(nz) for c in range(2)]
    line = [[at(x, y, z, c) for z in range(nz)] for x in range(nx) for y in range(4) for c in range(2)]
    return plane, line


def swap(x, axis, groups=None):
    return lax.all_to_all(
        x, axis, split_axis=0, concat_axis=0, axis_index_groups=groups, tiled=True
    )


def fold(x, n):
    return jnp.sum(x.reshape(n, x.shape[0] // n, x.shape[1]).astype(F32), axis=0).astype(BF16)


def sum_all(keep, send, groups):
    plane, line = groups
    n, m = len(plane[0]), len(line[0])
    x = (keep.astype(F32) + lax.ppermute(send, "frame", PARTNER).astype(F32)).astype(BF16)
    x = fold(swap(x, AXES, plane), n)
    x = fold(swap(jnp.tile(x, (m, 1)), AXES, line), m)
    x = swap(jnp.tile(x, (n, 1)), AXES, plane)
    return x, lax.ppermute(x, "frame", PARTNER)


def body(
    groups,
    features,
    vis_block,
    vis_count,
    query_frame,
    query_block,
    query_cell,
    cotangent,
    w_in,
    gain,
    w_qkv,
    w_out,
    w_head,
):
    outgoing = gather(vis_block, vis_count, query_frame, query_block, query_cell, features)
    arrived = swap(outgoing, "frame")
    ct = cotangent[0].reshape(4, 4, 8, 16).transpose(0, 1, 3, 2).reshape(4, TOK)
    ct = jnp.pad(ct, ((0, 12), (0, 0)))
    keep, send = token_grads(
        arrived,
        ct,
        jnp.concatenate([w_in, w_head, jnp.zeros((12, HID), BF16)]),
        gain.reshape(1, HID),
        w_qkv.T,
        w_qkv,
        w_out,
    )
    return unpack(*sum_all(keep, send, groups))


def solution(mesh):
    in_specs = (
        P("dp", "frame", None, None, None),
        P("dp", None, "frame", None),
        P("dp", None, "frame"),
        P("dp", None),
        P("dp", None),
        P("dp", None),
        P("dp", None, "frame", None),
        P(),
        P(),
        P(),
        P(),
        P(),
    )
    out_specs = (P(), P(), P(), P(), P())
    step = functools.partial(body, make_groups(mesh))
    return jax.shard_map(step, mesh=mesh, in_specs=in_specs, out_specs=out_specs, check_vma=False)
```

```python
import functools

import jax
import jax.numpy as jnp
from jax import lax
from jax.experimental import pallas as pl
from jax.experimental.pallas import tpu as pltpu
from jax.sharding import PartitionSpec as P

HEADS = 8
SIZE = 48
HID = 384
TOK = 512
HALF = 2560
F32 = jnp.float32
BF16 = jnp.bfloat16


def dot(left, right, dims=((1,), (0,))):
    return lax.dot_general(left, right, (dims, ((), ())), preferred_element_type=F32)


NT = ((1,), (1,))
TN = ((0,), (0,))


def gather_kernel(vis_ref, count_ref, qf_ref, qb_ref, qc_ref, feats_ref, *refs):
    outs, query_ref = refs[:8], refs[8]
    frame = lax.axis_index("frame")
    for s, out_ref in enumerate(outs):
        for gl in range(2):
            g = (frame ^ s) * 2 + gl
            for fr in range(2):
                shown = count_ref[0, fr, g]
                for k in range(2):
                    at = (gl * 2 + fr) * 128 + k * 64
                    tile = feats_ref[0, fr, vis_ref[0, fr, k, g]]
                    if k:
                        tile = jnp.where(shown > k, tile, jnp.zeros_like(tile))
                    out_ref[at : at + 64, :] = tile
    local = qf_ref[...] - frame * 2
    index = local * 2048 + qb_ref[...] * 64 + qc_ref[...]
    index = jnp.where((local >= 0) & (local < 2), index, -1)
    column = jnp.broadcast_to(index, (128, 256)).T[:, :1]
    query = jnp.zeros((256, 128), F32)
    for j in range(8):
        lanes = lax.broadcasted_iota(jnp.int32, (256, 512), 1) + j * 512
        chosen = jnp.where(lanes == column, 1.0, 0.0).astype(BF16)
        rows = feats_ref[0, j // 4, (j % 4) * 8 : (j % 4) * 8 + 8].reshape(512, 128)
        query = query + dot(chosen, rows)
    query_ref[...] = query.astype(BF16).reshape(8, 32, 128)
    for s, out_ref in enumerate(outs):
        out_ref[512:544, :] = query_ref[frame ^ s]


def gather(vis_block, vis_count, query_frame, query_block, query_cell, features):
    vm = pl.BlockSpec(memory_space=pltpu.VMEM)
    sm = pl.BlockSpec(memory_space=pltpu.SMEM)
    return pl.pallas_call(
        gather_kernel,
        out_shape=(jax.ShapeDtypeStruct((544, 128), BF16),) * 8,
        in_specs=[sm, sm, vm, vm, vm, vm],
        out_specs=(vm,) * 8,
        scratch_shapes=[pltpu.VMEM((8, 32, 128), BF16)],
        name="gather",
    )(
        vis_block.transpose(0, 2, 3, 1),
        vis_count.transpose(0, 2, 1),
        query_frame,
        query_block,
        query_cell,
        features,
    )


def token_kernel(*refs):
    token_body(refs[:8], *refs[8:])


def token_body(
    pieces,
    ct_ref,
    w_ends,
    gain_in,
    w_qkv_t,
    w_qkv,
    w_out,
    keep_ref,
    send_ref,
    corr32,
    corr16,
    x_zero,
    normed,
    left,
    qkv,
    d_y,
    d_mixed,
    right,
    inv_ref,
    g_in_ref,
    gain_ref,
    s_ref,
    t_ref,
    p_ref,
    d_ref,
):
    hidden, mixed = left.at[0], left.at[1]
    d_qkv, d_y16 = right.at[0:1152], right.at[1152:1536]
    frame = lax.axis_index("frame")
    core = frame % 2
    gain_ref[...] = jnp.broadcast_to(gain_in[...], (128, HID)).T
    query = sum(ref[512:544, :].astype(F32) for ref in pieces).astype(BF16)
    scale = 128 ** (-0.5)
    for s, ref in enumerate(pieces):
        first = pl.multiple_of((frame ^ s) * 16, 16)
        for g in range(2):
            part = dot(query[g * 16 : g * 16 + 16], ref[g * 256 : g * 256 + 256], NT) * scale
            for half in range(2):
                for fr in range(2):
                    row = pl.multiple_of(first + (g * 2 + half) * 128 + fr * 8, 8)
                    corr32[pl.ds(row, 8), :] = part[
                        half * 8 : half * 8 + 8, fr * 128 : fr * 128 + 128
                    ]
    corr16[...] = corr32[...].astype(BF16)

    ct = ct_ref[...]
    gain = gain_ref[...]
    for c in range(2):
        wide = slice(c * 256, c * 256 + 256)
        dy = dot(w_ends[128:144, :], ct[:, wide], TN)
        d_y[:, wide] = dy
        d_y16[:, wide] = dy.astype(BF16)
        d_mixed[:, wide] = dot(w_out[...], d_y16[:, wide]).astype(BF16)
        x_zero[:, wide] = dot(w_ends[0:128, :], corr16[wide, :], ((0,), (1,)))
        for n in range(2):
            cols = slice(c * 256 + n * 128, c * 256 + n * 128 + 128)
            x0 = x_zero[:, cols]
            centred = x0 - jnp.mean(x0, axis=0, keepdims=True)
            inv = lax.rsqrt(jnp.mean(centred * centred, axis=0, keepdims=True) + 1e-05)
            inv_ref[:, cols] = jnp.broadcast_to(inv, (8, 128))
            nrm = centred * inv
            normed[:, cols] = nrm
            hidden[:, cols] = (nrm * gain).astype(BF16)
        for r in range(3):
            rows = slice(r * 384, r * 384 + 384)
            qkv[rows, wide] = dot(w_qkv_t[rows, :], hidden[:, wide]).astype(BF16)

    own = (
        lax.broadcasted_iota(jnp.int32, (8, 128), 0)
        == lax.broadcasted_iota(jnp.int32, (8, 128), 1) % 8
    ).astype(F32)
    a_scale = SIZE ** (-0.5)
    e_scale = a_scale * 1.4426950408889634

    def block(b, carry):
        def cols(h):
            return pl.ds(pl.multiple_of((b * 2 + h // HEADS) * 128, 128), 128)

        def rows(h, n):
            at = n * HID + h % HEADS * SIZE
            return slice(at, at + SIZE)

        def scores(h):
            s_ref[h] = dot(qkv[rows(h, 1), cols(h)], qkv[rows(h, 0), cols(h)], TN)
            t_ref[h] = dot(qkv[rows(h, 2), cols(h)], d_mixed[rows(h, 0), cols(h)], TN).astype(BF16)

        def weights(h):
            score = s_ref[h].reshape(16, 8, 128)
            expo = jnp.exp2((score - jnp.max(score, axis=0, keepdims=True)) * e_scale)
            prob = expo * (own / jnp.sum(expo, axis=0))[None]
            p_ref[h] = prob.reshape(128, 128).astype(BF16)
            d_p = t_ref[h].astype(F32).reshape(16, 8, 128)
            inner = jnp.sum(d_p * prob, axis=0, keepdims=True)
            d_ref[h] = (prob * (d_p - inner)).reshape(128, 128).astype(BF16)

        def products(h):
            prob, d_s = p_ref[h], d_ref[h]
            mixed[rows(h, 0), cols(h)] = dot(qkv[rows(h, 2), cols(h)], prob).astype(BF16)
            d_v = dot(d_mixed[rows(h, 0), cols(h)], prob, NT)
            d_q = dot(qkv[rows(h, 1), cols(h)], d_s) * a_scale
            d_k = dot(qkv[rows(h, 0), cols(h)], d_s, NT) * a_scale
            d_qkv[rows(h, 0), cols(h)] = d_q.astype(BF16)
            d_qkv[rows(h, 1), cols(h)] = d_k.astype(BF16)
            d_qkv[rows(h, 2), cols(h)] = d_v.astype(BF16)

        for h in range(2 * HEADS + 4):
            if h < 2 * HEADS:
                scores(h)
            if 2 <= h < 2 * HEADS + 2:
                weights(h - 2)
            if h >= 4:
                products(h - 4)
        return carry

    lax.fori_loop(0, 2, block, 0)

    def pair_grads(ref, half, i):
        j = half * 2 + i
        rows = pl.ds(pl.multiple_of(j * HID, HID), HID)
        part = dot(left[jnp.where(j == 3, 1, 0)], right[rows, :], NT)
        for n in range(3):
            at = (i * 3 + n) * HID
            ref[at : at + HID, :] = part[:, n * 128 : n * 128 + 128].astype(BF16)

    head = jnp.zeros((16, HID), F32)
    gain_sum = jnp.zeros((HID, 128), F32)
    for c in range(2):
        wide = slice(c * 256, c * 256 + 256)
        y16 = (x_zero[:, wide] + dot(w_out[...], mixed[:, wide], TN)).astype(BF16)
        head = head + dot(ct[:, wide], y16, NT)
        x_zero[:, wide] = dot(w_qkv[...], d_qkv[:, wide])
        for n in range(2):
            cols = slice(c * 256 + n * 128, c * 256 + n * 128 + 128)
            pair_grads(*((send_ref, 1 - core, n), (keep_ref, core, n))[c])
            dh, nrm = x_zero[:, cols], normed[:, cols]
            gain_sum = gain_sum + dh * nrm
            dn = dh * gain
            m_one = jnp.mean(dn, axis=0, keepdims=True)
            m_two = jnp.mean(dn * nrm, axis=0, keepdims=True)
            dx = inv_ref[:1, cols] * (dn - m_one - nrm * m_two) + d_y[:, cols]
            d_mixed[:, cols] = dx.astype(BF16)
    g_in = dot(corr16[...], d_mixed[...], ((0,), (1,)))
    gain_row = jnp.sum(gain_sum.T, axis=0, keepdims=True)
    at_four = lax.broadcasted_iota(jnp.int32, (16, HID), 0) == 4
    head = jnp.where(at_four, jnp.broadcast_to(gain_row, (16, HID)), head)
    for j in range(3):
        g_in_ref[j * 128 : j * 128 + 128, :] = g_in[:, j * 128 : j * 128 + 128]
    for ref, half in ((keep_ref, core), (send_ref, 1 - core)):
        ref[2304:2496, :] = g_in_ref[pl.ds(pl.multiple_of(half * 192, 8), 192), :].astype(BF16)
        part = jnp.where(half == 0, head, 0.0).astype(BF16)
        for n in range(3):
            ref[2496 + n * 16 : 2512 + n * 16, :] = part[:, n * 128 : n * 128 + 128]
        ref[2544:HALF, :] = jnp.zeros((HALF - 2544, 128), BF16)


def token_grads(pieces, ct, w_ends, gain, w_qkv_t, w_qkv, w_out):
    vm = pl.BlockSpec(memory_space=pltpu.VMEM)
    half = jax.ShapeDtypeStruct((HALF, 128), BF16)
    return pl.pallas_call(
        token_kernel,
        out_shape=(half, half),
        in_specs=[vm] * 14,
        out_specs=(vm, vm),
        scratch_shapes=[
            pltpu.VMEM((TOK, 128), F32),
            pltpu.VMEM((TOK, 128), BF16),
            pltpu.VMEM((HID, TOK), F32),
            pltpu.VMEM((HID, TOK), F32),
            pltpu.VMEM((2, HID, TOK), BF16),
            pltpu.VMEM((3 * HID, TOK), BF16),
            pltpu.VMEM((HID, TOK), F32),
            pltpu.VMEM((HID, TOK), BF16),
            pltpu.VMEM((4 * HID, TOK), BF16),
            pltpu.VMEM((8, TOK), F32),
            pltpu.VMEM((HID, 128), F32),
            pltpu.VMEM((HID, 128), F32),
            pltpu.VMEM((2 * HEADS, 128, 128), F32),
            pltpu.VMEM((2 * HEADS, 128, 128), BF16),
            pltpu.VMEM((2 * HEADS, 128, 128), BF16),
            pltpu.VMEM((2 * HEADS, 128, 128), BF16),
        ],
        compiler_params=pltpu.CompilerParams(vmem_limit_bytes=28 << 20),
        name="token_grads",
    )(*pieces, ct, w_ends, gain, w_qkv_t, w_qkv, w_out)


def unpack_kernel(is_other, x_ref, *refs):
    g_in, g_gain, g_qkv, g_out, g_head, big, small, head32, gain32, sems = refs[-10:]
    half = lax.axis_index("frame") % 2
    if is_other:
        half = 1 - half

    def fill(j):
        for n in range(3):
            at = (j * 3 + n) * HID
            big[:, j * HID + n * 128 : j * HID + n * 128 + 128] = x_ref[at : at + HID, :].astype(F32)

    def copy(n, source, target):
        one = pltpu.make_async_copy(source, target, sems.at[n])
        one.start()
        return one

    @pl.when(half == 0)
    def _():
        fill(0)
        fill(1)
        copies = [copy(0, big, g_qkv.at[:, 0:768])]
        small[...] = x_ref[2304:2496, :].astype(F32)
        for n in range(3):
            tail = x_ref[2496 + n * 16 : 2512 + n * 16, :].astype(F32)
            head32[:, n * 128 : n * 128 + 128] = tail[:4]
            gain32[n * 128 : n * 128 + 128] = tail[4]
        copies.append(copy(1, small.at[0:128, :], g_in.at[:, 0:128]))
        copies.append(copy(2, small.at[128:192, :], g_in.at[0:64, 128:256]))
        copies.append(copy(3, head32, g_head))
        copies.append(copy(4, gain32, g_gain))
        for one in copies:
            one.wait()

    @pl.when(half == 1)
    def _():
        fill(0)
        copies = [copy(0, big.at[:, 0:384], g_qkv.at[:, 768:1152])]
        fill(1)
        copies.append(copy(1, big.at[:, 384:768], g_out))
        small[...] = x_ref[2304:2496, :].astype(F32)
        copies.append(copy(2, small.at[0:64, :], g_in.at[64:128, 128:256]))
        copies.append(copy(3, small.at[64:192, :], g_in.at[:, 256:384]))
        for one in copies:
            one.wait()


def unpack(is_other, x, done=()):
    hbm = pl.BlockSpec(memory_space=pl.ANY)
    shapes = ((128, HID), (HID,), (HID, 3 * HID), (HID, HID), (4, HID))
    return pl.pallas_call(
        functools.partial(unpack_kernel, is_other),
        out_shape=tuple(jax.ShapeDtypeStruct(shape, F32) for shape in shapes),
        in_specs=[pl.BlockSpec(memory_space=pltpu.VMEM)] + [hbm] * len(done),
        out_specs=(hbm,) * 5,
        scratch_shapes=[
            pltpu.VMEM((HID, 2 * HID), F32),
            pltpu.VMEM((192, 128), F32),
            pltpu.VMEM((4, HID), F32),
            pltpu.VMEM((HID,), F32),
            pltpu.SemaphoreType.DMA((5,)),
        ],
        input_output_aliases={i + 1: i for i in range(len(done))},
        compiler_params=pltpu.CompilerParams(vmem_limit_bytes=12 << 20),
        cost_estimate=pl.CostEstimate(flops=0, transcendentals=0, bytes_accessed=2 << 20),
        name="unpack_other" if is_other else "unpack_own",
    )(x, *done)


AXES = ("dp", "frame")
PARTNER = [(i, i ^ 1) for i in range(8)]


def make_groups(mesh):
    nx = max(mesh.shape["dp"] // 8, 1)
    nz = mesh.shape["dp"] // nx
    at = lambda x, y, z, c: (x * nz + z) * 8 + y * 2 + c
    plane = [[at(x, y, z, c) for y in range(4) for x in range(nx)] for z in range(nz) for c in range(2)]
    line = [[at(x, y, z, c) for z in range(nz)] for x in range(nx) for y in range(4) for c in range(2)]
    return plane, line


def swap(x, axis, groups=None):
    return lax.all_to_all(
        x, axis, split_axis=0, concat_axis=0, axis_index_groups=groups, tiled=True
    )


def fold(x, n):
    return jnp.sum(x.reshape(n, x.shape[0] // n, x.shape[1]).astype(F32), axis=0).astype(BF16)


def sum_all(keep, send, groups):
    plane, line = groups
    n, m = len(plane[0]), len(line[0])
    x = (keep.astype(F32) + lax.ppermute(send, "frame", PARTNER).astype(F32)).astype(BF16)
    x = fold(swap(x, AXES, plane), n)
    x = fold(swap(jnp.tile(x, (m, 1)), AXES, line), m)
    x = swap(jnp.tile(x, (n, 1)), AXES, plane)
    return x, lax.ppermute(x, "frame", PARTNER)


def body(
    groups,
    features,
    vis_block,
    vis_count,
    query_frame,
    query_block,
    query_cell,
    cotangent,
    w_in,
    gain,
    w_qkv,
    w_out,
    w_head,
):
    outgoing = gather(vis_block, vis_count, query_frame, query_block, query_cell, features)
    pieces = {0: outgoing[0]}
    for s in (4, 5, 2, 3, 6, 7, 1):
        pieces[s] = lax.ppermute(outgoing[s], "frame", [(i, i ^ s) for i in range(8)])
    arrived = [pieces[s] for s in range(8)]
    ct = cotangent[0].reshape(4, 4, 8, 16).transpose(0, 1, 3, 2).reshape(4, TOK)
    ct = jnp.pad(ct, ((0, 12), (0, 0)))
    keep, send = token_grads(
        arrived,
        ct,
        jnp.concatenate([w_in, w_head, jnp.zeros((12, HID), BF16)]),
        gain.reshape(1, HID),
        w_qkv.T,
        w_qkv,
        w_out,
    )
    own, other = sum_all(keep, send, groups)
    return unpack(True, other, unpack(False, own))


def solution(mesh):
    in_specs = (
        P("dp", "frame", None, None, None),
        P("dp", None, "frame", None),
        P("dp", None, "frame"),
        P("dp", None),
        P("dp", None),
        P("dp", None),
        P("dp", None, "frame", None),
        P(),
        P(),
        P(),
        P(),
        P(),
    )
    out_specs = (P(), P(), P(), P(), P())
    step = functools.partial(body, make_groups(mesh))
    return jax.shard_map(step, mesh=mesh, in_specs=in_specs, out_specs=out_specs, check_vma=False)
```

```python
import functools

import jax
import jax.numpy as jnp
from jax import lax
from jax.experimental import pallas as pl
from jax.experimental.pallas import tpu as pltpu
from jax.sharding import PartitionSpec as P

HEADS = 8
SIZE = 48
HID = 384
TOK = 512
ORDER = (4, 5, 2, 3, 6, 7, 1, 0)
HALF = 2560
F32 = jnp.float32
BF16 = jnp.bfloat16


def dot(left, right, dims=((1,), (0,))):
    return lax.dot_general(left, right, (dims, ((), ())), preferred_element_type=F32)


NT = ((1,), (1,))
TN = ((0,), (0,))


def gather_kernel(vis_ref, count_ref, qf_ref, qb_ref, qc_ref, feats_ref, *refs):
    outs, query_ref = refs[:8], refs[8]
    frame = lax.axis_index("frame")
    for s, out_ref in enumerate(outs):
        for gl in range(2):
            g = (frame ^ s) * 2 + gl
            for fr in range(2):
                shown = count_ref[0, fr, g]
                for k in range(2):
                    at = (gl * 2 + fr) * 128 + k * 64
                    tile = feats_ref[0, fr, vis_ref[0, fr, k, g]]
                    if k:
                        tile = jnp.where(shown > k, tile, jnp.zeros_like(tile))
                    out_ref[at : at + 64, :] = tile
    local = qf_ref[...] - frame * 2
    index = local * 2048 + qb_ref[...] * 64 + qc_ref[...]
    index = jnp.where((local >= 0) & (local < 2), index, -1)
    column = jnp.broadcast_to(index, (128, 256)).T[:, :1]
    query = jnp.zeros((256, 128), F32)
    for j in range(8):
        lanes = lax.broadcasted_iota(jnp.int32, (256, 512), 1) + j * 512
        chosen = jnp.where(lanes == column, 1.0, 0.0).astype(BF16)
        rows = feats_ref[0, j // 4, (j % 4) * 8 : (j % 4) * 8 + 8].reshape(512, 128)
        query = query + dot(chosen, rows)
    query_ref[...] = query.astype(BF16).reshape(8, 32, 128)
    for s, out_ref in enumerate(outs):
        out_ref[512:544, :] = query_ref[frame ^ s]


def gather(vis_block, vis_count, query_frame, query_block, query_cell, features):
    vm = pl.BlockSpec(memory_space=pltpu.VMEM)
    sm = pl.BlockSpec(memory_space=pltpu.SMEM)
    return pl.pallas_call(
        gather_kernel,
        out_shape=(jax.ShapeDtypeStruct((544, 128), BF16),) * 8,
        in_specs=[sm, sm, vm, vm, vm, vm],
        out_specs=(vm,) * 8,
        scratch_shapes=[pltpu.VMEM((8, 32, 128), BF16)],
        name="gather",
    )(
        vis_block.transpose(0, 2, 3, 1),
        vis_count.transpose(0, 2, 1),
        query_frame,
        query_block,
        query_cell,
        features,
    )


def token_kernel(*refs):
    token_body(refs[:8], *refs[8:])


def token_body(
    pieces,
    ct_ref,
    w_ends,
    gain_in,
    w_qkv_t,
    w_qkv,
    w_out,
    keep_ref,
    send_ref,
    corr32,
    corr16,
    x_zero,
    normed,
    left,
    qkv,
    d_y,
    d_mixed,
    right,
    inv_ref,
    g_in_ref,
    gain_ref,
    s_ref,
    t_ref,
    p_ref,
    d_ref,
):
    hidden, mixed = left.at[0], left.at[1]
    d_qkv, d_y16 = right.at[0:1152], right.at[1152:1536]
    frame = lax.axis_index("frame")
    core = frame % 2
    gain_ref[...] = jnp.broadcast_to(gain_in[...], (128, HID)).T
    query = sum(ref[512:544, :].astype(F32) for ref in pieces).astype(BF16)
    scale = 128 ** (-0.5)
    for s, ref in zip(ORDER, pieces):
        first = pl.multiple_of((frame ^ s) * 16, 16)
        for g in range(2):
            part = dot(query[g * 16 : g * 16 + 16], ref[g * 256 : g * 256 + 256], NT) * scale
            for half in range(2):
                for fr in range(2):
                    row = pl.multiple_of(first + (g * 2 + half) * 128 + fr * 8, 8)
                    corr32[pl.ds(row, 8), :] = part[
                        half * 8 : half * 8 + 8, fr * 128 : fr * 128 + 128
                    ]
    corr16[...] = corr32[...].astype(BF16)

    ct = ct_ref[...]
    gain = gain_ref[...]
    for c in range(2):
        wide = slice(c * 256, c * 256 + 256)
        dy = dot(w_ends[128:144, :], ct[:, wide], TN)
        d_y[:, wide] = dy
        d_y16[:, wide] = dy.astype(BF16)
        d_mixed[:, wide] = dot(w_out[...], d_y16[:, wide]).astype(BF16)
        x_zero[:, wide] = dot(w_ends[0:128, :], corr16[wide, :], ((0,), (1,)))
        for n in range(2):
            cols = slice(c * 256 + n * 128, c * 256 + n * 128 + 128)
            x0 = x_zero[:, cols]
            centred = x0 - jnp.mean(x0, axis=0, keepdims=True)
            inv = lax.rsqrt(jnp.mean(centred * centred, axis=0, keepdims=True) + 1e-05)
            inv_ref[:, cols] = jnp.broadcast_to(inv, (8, 128))
            nrm = centred * inv
            normed[:, cols] = nrm
            hidden[:, cols] = (nrm * gain).astype(BF16)
        for r in range(3):
            rows = slice(r * 384, r * 384 + 384)
            qkv[rows, wide] = dot(w_qkv_t[rows, :], hidden[:, wide]).astype(BF16)

    own = (
        lax.broadcasted_iota(jnp.int32, (8, 128), 0)
        == lax.broadcasted_iota(jnp.int32, (8, 128), 1) % 8
    ).astype(F32)
    a_scale = SIZE ** (-0.5)
    e_scale = a_scale * 1.4426950408889634

    def block(b, carry):
        def cols(h):
            return pl.ds(pl.multiple_of((b * 2 + h // HEADS) * 128, 128), 128)

        def rows(h, n):
            at = n * HID + h % HEADS * SIZE
            return slice(at, at + SIZE)

        def scores(h):
            s_ref[h] = dot(qkv[rows(h, 1), cols(h)], qkv[rows(h, 0), cols(h)], TN)
            t_ref[h] = dot(qkv[rows(h, 2), cols(h)], d_mixed[rows(h, 0), cols(h)], TN).astype(BF16)

        def weights(h):
            score = s_ref[h].reshape(16, 8, 128)
            expo = jnp.exp2((score - jnp.max(score, axis=0, keepdims=True)) * e_scale)
            prob = expo * (own / jnp.sum(expo, axis=0))[None]
            p_ref[h] = prob.reshape(128, 128).astype(BF16)
            d_p = t_ref[h].astype(F32).reshape(16, 8, 128)
            inner = jnp.sum(d_p * prob, axis=0, keepdims=True)
            d_ref[h] = (prob * (d_p - inner)).reshape(128, 128).astype(BF16)

        def products(h):
            prob, d_s = p_ref[h], d_ref[h]
            mixed[rows(h, 0), cols(h)] = dot(qkv[rows(h, 2), cols(h)], prob).astype(BF16)
            d_v = dot(d_mixed[rows(h, 0), cols(h)], prob, NT)
            d_q = dot(qkv[rows(h, 1), cols(h)], d_s) * a_scale
            d_k = dot(qkv[rows(h, 0), cols(h)], d_s, NT) * a_scale
            d_qkv[rows(h, 0), cols(h)] = d_q.astype(BF16)
            d_qkv[rows(h, 1), cols(h)] = d_k.astype(BF16)
            d_qkv[rows(h, 2), cols(h)] = d_v.astype(BF16)

        for h in range(2 * HEADS + 4):
            if h < 2 * HEADS:
                scores(h)
            if 2 <= h < 2 * HEADS + 2:
                weights(h - 2)
            if h >= 4:
                products(h - 4)
        return carry

    lax.fori_loop(0, 2, block, 0)

    def pair_grads(ref, half, i):
        j = half * 2 + i
        rows = pl.ds(pl.multiple_of(j * HID, HID), HID)
        part = dot(left[jnp.where(j == 3, 1, 0)], right[rows, :], NT)
        for n in range(3):
            at = (i * 3 + n) * HID
            ref[at : at + HID, :] = part[:, n * 128 : n * 128 + 128].astype(BF16)

    head = jnp.zeros((16, HID), F32)
    gain_sum = jnp.zeros((HID, 128), F32)
    for c in range(2):
        wide = slice(c * 256, c * 256 + 256)
        y16 = (x_zero[:, wide] + dot(w_out[...], mixed[:, wide], TN)).astype(BF16)
        head = head + dot(ct[:, wide], y16, NT)
        x_zero[:, wide] = dot(w_qkv[...], d_qkv[:, wide])
        for n in range(2):
            cols = slice(c * 256 + n * 128, c * 256 + n * 128 + 128)
            pair_grads(*((send_ref, 1 - core, n), (keep_ref, core, n))[c])
            dh, nrm = x_zero[:, cols], normed[:, cols]
            gain_sum = gain_sum + dh * nrm
            dn = dh * gain
            m_one = jnp.mean(dn, axis=0, keepdims=True)
            m_two = jnp.mean(dn * nrm, axis=0, keepdims=True)
            dx = inv_ref[:1, cols] * (dn - m_one - nrm * m_two) + d_y[:, cols]
            d_mixed[:, cols] = dx.astype(BF16)
    g_in = dot(corr16[...], d_mixed[...], ((0,), (1,)))
    gain_row = jnp.sum(gain_sum.T, axis=0, keepdims=True)
    at_four = lax.broadcasted_iota(jnp.int32, (16, HID), 0) == 4
    head = jnp.where(at_four, jnp.broadcast_to(gain_row, (16, HID)), head)
    for j in range(3):
        g_in_ref[j * 128 : j * 128 + 128, :] = g_in[:, j * 128 : j * 128 + 128]
    for ref, half in ((keep_ref, core), (send_ref, 1 - core)):
        ref[2304:2496, :] = g_in_ref[pl.ds(pl.multiple_of(half * 192, 8), 192), :].astype(BF16)
        part = jnp.where(half == 0, head, 0.0).astype(BF16)
        for n in range(3):
            ref[2496 + n * 16 : 2512 + n * 16, :] = part[:, n * 128 : n * 128 + 128]
        ref[2544:HALF, :] = jnp.zeros((HALF - 2544, 128), BF16)


def token_grads(pieces, ct, w_ends, gain, w_qkv_t, w_qkv, w_out):
    vm = pl.BlockSpec(memory_space=pltpu.VMEM)
    half = jax.ShapeDtypeStruct((HALF, 128), BF16)
    return pl.pallas_call(
        token_kernel,
        out_shape=(half, half),
        in_specs=[vm] * 14,
        out_specs=(vm, vm),
        scratch_shapes=[
            pltpu.VMEM((TOK, 128), F32),
            pltpu.VMEM((TOK, 128), BF16),
            pltpu.VMEM((HID, TOK), F32),
            pltpu.VMEM((HID, TOK), F32),
            pltpu.VMEM((2, HID, TOK), BF16),
            pltpu.VMEM((3 * HID, TOK), BF16),
            pltpu.VMEM((HID, TOK), F32),
            pltpu.VMEM((HID, TOK), BF16),
            pltpu.VMEM((4 * HID, TOK), BF16),
            pltpu.VMEM((8, TOK), F32),
            pltpu.VMEM((HID, 128), F32),
            pltpu.VMEM((HID, 128), F32),
            pltpu.VMEM((2 * HEADS, 128, 128), F32),
            pltpu.VMEM((2 * HEADS, 128, 128), BF16),
            pltpu.VMEM((2 * HEADS, 128, 128), BF16),
            pltpu.VMEM((2 * HEADS, 128, 128), BF16),
        ],
        compiler_params=pltpu.CompilerParams(vmem_limit_bytes=28 << 20),
        name="token_grads",
    )(*pieces, ct, w_ends, gain, w_qkv_t, w_qkv, w_out)


def unpack_kernel(is_other, x_ref, *refs):
    g_in, g_gain, g_qkv, g_out, g_head, big, small, head32, gain32, sems = refs[-10:]
    half = lax.axis_index("frame") % 2
    if is_other:
        half = 1 - half

    def fill(j):
        for n in range(3):
            at = (j * 3 + n) * HID
            big[:, j * HID + n * 128 : j * HID + n * 128 + 128] = x_ref[at : at + HID, :].astype(F32)

    def copy(n, source, target):
        one = pltpu.make_async_copy(source, target, sems.at[n])
        one.start()
        return one

    @pl.when(half == 0)
    def _():
        fill(0)
        fill(1)
        copies = [copy(0, big, g_qkv.at[:, 0:768])]
        small[...] = x_ref[2304:2496, :].astype(F32)
        for n in range(3):
            tail = x_ref[2496 + n * 16 : 2512 + n * 16, :].astype(F32)
            head32[:, n * 128 : n * 128 + 128] = tail[:4]
            gain32[n * 128 : n * 128 + 128] = tail[4]
        copies.append(copy(1, small.at[0:128, :], g_in.at[:, 0:128]))
        copies.append(copy(2, small.at[128:192, :], g_in.at[0:64, 128:256]))
        copies.append(copy(3, head32, g_head))
        copies.append(copy(4, gain32, g_gain))
        for one in copies:
            one.wait()

    @pl.when(half == 1)
    def _():
        fill(0)
        copies = [copy(0, big.at[:, 0:384], g_qkv.at[:, 768:1152])]
        fill(1)
        copies.append(copy(1, big.at[:, 384:768], g_out))
        small[...] = x_ref[2304:2496, :].astype(F32)
        copies.append(copy(2, small.at[0:64, :], g_in.at[64:128, 128:256]))
        copies.append(copy(3, small.at[64:192, :], g_in.at[:, 256:384]))
        for one in copies:
            one.wait()


def unpack(is_other, x, done=()):
    hbm = pl.BlockSpec(memory_space=pl.ANY)
    shapes = ((128, HID), (HID,), (HID, 3 * HID), (HID, HID), (4, HID))
    return pl.pallas_call(
        functools.partial(unpack_kernel, is_other),
        out_shape=tuple(jax.ShapeDtypeStruct(shape, F32) for shape in shapes),
        in_specs=[pl.BlockSpec(memory_space=pltpu.VMEM)] + [hbm] * len(done),
        out_specs=(hbm,) * 5,
        scratch_shapes=[
            pltpu.VMEM((HID, 2 * HID), F32),
            pltpu.VMEM((192, 128), F32),
            pltpu.VMEM((4, HID), F32),
            pltpu.VMEM((HID,), F32),
            pltpu.SemaphoreType.DMA((5,)),
        ],
        input_output_aliases={i + 1: i for i in range(len(done))},
        compiler_params=pltpu.CompilerParams(vmem_limit_bytes=12 << 20),
        cost_estimate=pl.CostEstimate(flops=0, transcendentals=0, bytes_accessed=2 << 20),
        name="unpack_other" if is_other else "unpack_own",
    )(x, *done)


AXES = ("dp", "frame")
PARTNER = [(i, i ^ 1) for i in range(8)]


def make_groups(mesh):
    nx = max(mesh.shape["dp"] // 8, 1)
    nz = mesh.shape["dp"] // nx
    at = lambda x, y, z, c: (x * nz + z) * 8 + y * 2 + c
    plane = [[at(x, y, z, c) for y in range(4) for x in range(nx)] for z in range(nz) for c in range(2)]
    line = [[at(x, y, z, c) for z in range(nz)] for x in range(nx) for y in range(4) for c in range(2)]
    return plane, line


def swap(x, axis, groups=None):
    return lax.all_to_all(
        x, axis, split_axis=0, concat_axis=0, axis_index_groups=groups, tiled=True
    )


def fold(x, n):
    return jnp.sum(x.reshape(n, x.shape[0] // n, x.shape[1]).astype(F32), axis=0).astype(BF16)


def sum_all(keep, send, groups):
    plane, line = groups
    n, m = len(plane[0]), len(line[0])
    x = (keep.astype(F32) + lax.ppermute(send, "frame", PARTNER).astype(F32)).astype(BF16)
    x = fold(swap(x, AXES, plane), n)
    x = fold(swap(jnp.tile(x, (m, 1)), AXES, line), m)
    x = swap(jnp.tile(x, (n, 1)), AXES, plane)
    return x, lax.ppermute(x, "frame", PARTNER)


def body(
    groups,
    features,
    vis_block,
    vis_count,
    query_frame,
    query_block,
    query_cell,
    cotangent,
    w_in,
    gain,
    w_qkv,
    w_out,
    w_head,
):
    outgoing = gather(vis_block, vis_count, query_frame, query_block, query_cell, features)
    arrived = [
        lax.ppermute(outgoing[s], "frame", [(i, i ^ s) for i in range(8)]) if s else outgoing[0]
        for s in ORDER
    ]
    ct = cotangent[0].reshape(4, 4, 8, 16).transpose(0, 1, 3, 2).reshape(4, TOK)
    ct = jnp.pad(ct, ((0, 12), (0, 0)))
    keep, send = token_grads(
        arrived,
        ct,
        jnp.concatenate([w_in, w_head, jnp.zeros((12, HID), BF16)]),
        gain.reshape(1, HID),
        w_qkv.T,
        w_qkv,
        w_out,
    )
    own, other = sum_all(keep, send, groups)
    return unpack(True, other, unpack(False, own))


def solution(mesh):
    in_specs = (
        P("dp", "frame", None, None, None),
        P("dp", None, "frame", None),
        P("dp", None, "frame"),
        P("dp", None),
        P("dp", None),
        P("dp", None),
        P("dp", None, "frame", None),
        P(),
        P(),
        P(),
        P(),
        P(),
    )
    out_specs = (P(), P(), P(), P(), P())
    step = functools.partial(body, make_groups(mesh))
    return jax.shard_map(step, mesh=mesh, in_specs=in_specs, out_specs=out_specs, check_vma=False)
```

```python
import functools

import jax
import jax.numpy as jnp
from jax import lax
from jax.experimental import pallas as pl
from jax.experimental.pallas import tpu as pltpu
from jax.sharding import PartitionSpec as P

HEADS = 8
SIZE = 48
HID = 384
TOK = 512
ORDER = (4, 5, 2, 3, 6, 7, 1, 0)
HALF = 2560
F32 = jnp.float32
BF16 = jnp.bfloat16


def dot(left, right, dims=((1,), (0,))):
    return lax.dot_general(left, right, (dims, ((), ())), preferred_element_type=F32)


NT = ((1,), (1,))
TN = ((0,), (0,))


def gather_kernel(vis_ref, count_ref, qf_ref, qb_ref, qc_ref, feats_hbm, *refs):
    outs, (feats_ref, rows_ref, query_ref, in_sems, out_sems) = refs[:8], refs[8:]
    loads = [
        pltpu.make_async_copy(feats_hbm.at[0, fr], feats_ref.at[fr], in_sems.at[fr]) for fr in range(2)
    ]
    for load in loads:
        load.start()
    frame = lax.axis_index("frame")
    local = qf_ref[...] - frame * 2
    index = local * 2048 + qb_ref[...] * 64 + qc_ref[...]
    index = jnp.where((local >= 0) & (local < 2), index, -1)
    column = jnp.broadcast_to(index, (128, 256)).T[:, :1]
    stores = []
    for fr in range(2):
        loads[fr].wait()
        for s in range(8):
            for gl in range(2):
                g = (frame ^ s) * 2 + gl
                shown = count_ref[0, fr, g]
                for k in range(2):
                    at = (gl * 2 + fr) * 128 + k * 64
                    tile = feats_ref[fr, vis_ref[0, fr, k, g]]
                    if k:
                        tile = jnp.where(shown > k, tile, jnp.zeros_like(tile))
                    rows_ref[s, at : at + 64, :] = tile
            if fr:
                stores.append(
                    pltpu.make_async_copy(rows_ref.at[s], outs[s].at[0:512, :], out_sems.at[s])
                )
                stores[-1].start()
    query = jnp.zeros((256, 128), F32)
    for j in range(8):
        lanes = lax.broadcasted_iota(jnp.int32, (256, 512), 1) + j * 512
        chosen = jnp.where(lanes == column, 1.0, 0.0).astype(BF16)
        rows = feats_ref[j // 4, (j % 4) * 8 : (j % 4) * 8 + 8].reshape(512, 128)
        query = query + dot(chosen, rows)
    query_ref[...] = query.astype(BF16).reshape(8, 32, 128)
    for s in range(8):
        stores.append(
            pltpu.make_async_copy(query_ref.at[frame ^ s], outs[s].at[512:544, :], out_sems.at[8 + s])
        )
        stores[-1].start()
    for store in stores:
        store.wait()


def gather(vis_block, vis_count, query_frame, query_block, query_cell, features):
    vm = pl.BlockSpec(memory_space=pltpu.VMEM)
    sm = pl.BlockSpec(memory_space=pltpu.SMEM)
    hbm = pl.BlockSpec(memory_space=pl.ANY)
    return pl.pallas_call(
        gather_kernel,
        out_shape=(jax.ShapeDtypeStruct((544, 128), BF16),) * 8,
        in_specs=[sm, sm, vm, vm, vm, hbm],
        out_specs=(hbm,) * 8,
        scratch_shapes=[
            pltpu.VMEM((2, 32, 64, 128), BF16),
            pltpu.VMEM((8, 512, 128), BF16),
            pltpu.VMEM((8, 32, 128), BF16),
            pltpu.SemaphoreType.DMA((2,)),
            pltpu.SemaphoreType.DMA((16,)),
        ],
        name="gather",
    )(
        vis_block.transpose(0, 2, 3, 1),
        vis_count.transpose(0, 2, 1),
        query_frame,
        query_block,
        query_cell,
        features,
    )


def token_kernel(*refs):
    token_body(refs[:8], *refs[8:])


def token_body(
    pieces,
    ct_ref,
    w_ends,
    gain_in,
    w_qkv_t,
    w_qkv,
    w_out,
    keep_ref,
    send_ref,
    corr32,
    corr16,
    x_zero,
    normed,
    left,
    qkv,
    d_y,
    d_mixed,
    right,
    inv_ref,
    g_in_ref,
    gain_ref,
    s_ref,
    t_ref,
    p_ref,
    d_ref,
):
    hidden, mixed = left.at[0], left.at[1]
    d_qkv, d_y16 = right.at[0:1152], right.at[1152:1536]
    frame = lax.axis_index("frame")
    core = frame % 2
    gain_ref[...] = jnp.broadcast_to(gain_in[...], (128, HID)).T
    query = sum(ref[512:544, :].astype(F32) for ref in pieces).astype(BF16)
    scale = 128 ** (-0.5)
    for s, ref in zip(ORDER, pieces):
        first = pl.multiple_of((frame ^ s) * 16, 16)
        for g in range(2):
            part = dot(query[g * 16 : g * 16 + 16], ref[g * 256 : g * 256 + 256], NT) * scale
            for half in range(2):
                for fr in range(2):
                    row = pl.multiple_of(first + (g * 2 + half) * 128 + fr * 8, 8)
                    corr32[pl.ds(row, 8), :] = part[
                        half * 8 : half * 8 + 8, fr * 128 : fr * 128 + 128
                    ]
    corr16[...] = corr32[...].astype(BF16)

    ct = ct_ref[...]
    gain = gain_ref[...]
    for c in range(2):
        wide = slice(c * 256, c * 256 + 256)
        dy = dot(w_ends[128:144, :], ct[:, wide], TN)
        d_y[:, wide] = dy
        d_y16[:, wide] = dy.astype(BF16)
        d_mixed[:, wide] = dot(w_out[...], d_y16[:, wide]).astype(BF16)
        x_zero[:, wide] = dot(w_ends[0:128, :], corr16[wide, :], ((0,), (1,)))
        for n in range(2):
            cols = slice(c * 256 + n * 128, c * 256 + n * 128 + 128)
            x0 = x_zero[:, cols]
            centred = x0 - jnp.mean(x0, axis=0, keepdims=True)
            inv = lax.rsqrt(jnp.mean(centred * centred, axis=0, keepdims=True) + 1e-05)
            inv_ref[:, cols] = jnp.broadcast_to(inv, (8, 128))
            nrm = centred * inv
            normed[:, cols] = nrm
            hidden[:, cols] = (nrm * gain).astype(BF16)
        for r in range(3):
            rows = slice(r * 384, r * 384 + 384)
            qkv[rows, wide] = dot(w_qkv_t[rows, :], hidden[:, wide]).astype(BF16)

    own = (
        lax.broadcasted_iota(jnp.int32, (8, 128), 0)
        == lax.broadcasted_iota(jnp.int32, (8, 128), 1) % 8
    ).astype(F32)
    a_scale = SIZE ** (-0.5)
    e_scale = a_scale * 1.4426950408889634

    def block(b, carry):
        def cols(h):
            return pl.ds(pl.multiple_of((b * 2 + h // HEADS) * 128, 128), 128)

        def rows(h, n):
            at = n * HID + h % HEADS * SIZE
            return slice(at, at + SIZE)

        def scores(h):
            s_ref[h] = dot(qkv[rows(h, 1), cols(h)], qkv[rows(h, 0), cols(h)], TN)
            t_ref[h] = dot(qkv[rows(h, 2), cols(h)], d_mixed[rows(h, 0), cols(h)], TN).astype(BF16)

        def weights(h):
            score = s_ref[h].reshape(16, 8, 128)
            expo = jnp.exp2((score - jnp.max(score, axis=0, keepdims=True)) * e_scale)
            prob = expo * (own / jnp.sum(expo, axis=0))[None]
            p_ref[h] = prob.reshape(128, 128).astype(BF16)
            d_p = t_ref[h].astype(F32).reshape(16, 8, 128)
            inner = jnp.sum(d_p * prob, axis=0, keepdims=True)
            d_ref[h] = (prob * (d_p - inner)).reshape(128, 128).astype(BF16)

        def products(h):
            prob, d_s = p_ref[h], d_ref[h]
            mixed[rows(h, 0), cols(h)] = dot(qkv[rows(h, 2), cols(h)], prob).astype(BF16)
            d_v = dot(d_mixed[rows(h, 0), cols(h)], prob, NT)
            d_q = dot(qkv[rows(h, 1), cols(h)], d_s) * a_scale
            d_k = dot(qkv[rows(h, 0), cols(h)], d_s, NT) * a_scale
            d_qkv[rows(h, 0), cols(h)] = d_q.astype(BF16)
            d_qkv[rows(h, 1), cols(h)] = d_k.astype(BF16)
            d_qkv[rows(h, 2), cols(h)] = d_v.astype(BF16)

        for h in range(2 * HEADS + 4):
            if h < 2 * HEADS:
                scores(h)
            if 2 <= h < 2 * HEADS + 2:
                weights(h - 2)
            if h >= 4:
                products(h - 4)
        return carry

    lax.fori_loop(0, 2, block, 0)

    def pair_grads(ref, half, i):
        j = half * 2 + i
        rows = pl.ds(pl.multiple_of(j * HID, HID), HID)
        part = dot(left[jnp.where(j == 3, 1, 0)], right[rows, :], NT)
        for n in range(3):
            at = (i * 3 + n) * HID
            ref[at : at + HID, :] = part[:, n * 128 : n * 128 + 128].astype(BF16)

    head = jnp.zeros((16, HID), F32)
    gain_sum = jnp.zeros((HID, 128), F32)
    for c in range(2):
        wide = slice(c * 256, c * 256 + 256)
        y16 = (x_zero[:, wide] + dot(w_out[...], mixed[:, wide], TN)).astype(BF16)
        head = head + dot(ct[:, wide], y16, NT)
        x_zero[:, wide] = dot(w_qkv[...], d_qkv[:, wide])
        for n in range(2):
            cols = slice(c * 256 + n * 128, c * 256 + n * 128 + 128)
            pair_grads(*((send_ref, 1 - core, n), (keep_ref, core, n))[c])
            dh, nrm = x_zero[:, cols], normed[:, cols]
            gain_sum = gain_sum + dh * nrm
            dn = dh * gain
            m_one = jnp.mean(dn, axis=0, keepdims=True)
            m_two = jnp.mean(dn * nrm, axis=0, keepdims=True)
            dx = inv_ref[:1, cols] * (dn - m_one - nrm * m_two) + d_y[:, cols]
            d_mixed[:, cols] = dx.astype(BF16)
    g_in = dot(corr16[...], d_mixed[...], ((0,), (1,)))
    gain_row = jnp.sum(gain_sum.T, axis=0, keepdims=True)
    at_four = lax.broadcasted_iota(jnp.int32, (16, HID), 0) == 4
    head = jnp.where(at_four, jnp.broadcast_to(gain_row, (16, HID)), head)
    for j in range(3):
        g_in_ref[j * 128 : j * 128 + 128, :] = g_in[:, j * 128 : j * 128 + 128]
    for ref, half in ((keep_ref, core), (send_ref, 1 - core)):
        ref[2304:2496, :] = g_in_ref[pl.ds(pl.multiple_of(half * 192, 8), 192), :].astype(BF16)
        part = jnp.where(half == 0, head, 0.0).astype(BF16)
        for n in range(3):
            ref[2496 + n * 16 : 2512 + n * 16, :] = part[:, n * 128 : n * 128 + 128]
        ref[2544:HALF, :] = jnp.zeros((HALF - 2544, 128), BF16)


def token_grads(pieces, ct, w_ends, gain, w_qkv_t, w_qkv, w_out):
    vm = pl.BlockSpec(memory_space=pltpu.VMEM)
    half = jax.ShapeDtypeStruct((HALF, 128), BF16)
    return pl.pallas_call(
        token_kernel,
        out_shape=(half, half),
        in_specs=[vm] * 14,
        out_specs=(vm, vm),
        scratch_shapes=[
            pltpu.VMEM((TOK, 128), F32),
            pltpu.VMEM((TOK, 128), BF16),
            pltpu.VMEM((HID, TOK), F32),
            pltpu.VMEM((HID, TOK), F32),
            pltpu.VMEM((2, HID, TOK), BF16),
            pltpu.VMEM((3 * HID, TOK), BF16),
            pltpu.VMEM((HID, TOK), F32),
            pltpu.VMEM((HID, TOK), BF16),
            pltpu.VMEM((4 * HID, TOK), BF16),
            pltpu.VMEM((8, TOK), F32),
            pltpu.VMEM((HID, 128), F32),
            pltpu.VMEM((HID, 128), F32),
            pltpu.VMEM((2 * HEADS, 128, 128), F32),
            pltpu.VMEM((2 * HEADS, 128, 128), BF16),
            pltpu.VMEM((2 * HEADS, 128, 128), BF16),
            pltpu.VMEM((2 * HEADS, 128, 128), BF16),
        ],
        compiler_params=pltpu.CompilerParams(vmem_limit_bytes=28 << 20),
        name="token_grads",
    )(*pieces, ct, w_ends, gain, w_qkv_t, w_qkv, w_out)


def unpack_kernel(is_other, x_ref, *refs):
    g_in, g_gain, g_qkv, g_out, g_head, big, small, head32, gain32, sems = refs[-10:]
    half = lax.axis_index("frame") % 2
    if is_other:
        half = 1 - half

    def fill(j):
        for n in range(3):
            at = (j * 3 + n) * HID
            big[:, j * HID + n * 128 : j * HID + n * 128 + 128] = x_ref[at : at + HID, :].astype(F32)

    def copy(n, source, target):
        one = pltpu.make_async_copy(source, target, sems.at[n])
        one.start()
        return one

    @pl.when(half == 0)
    def _():
        fill(0)
        fill(1)
        copies = [copy(0, big, g_qkv.at[:, 0:768])]
        small[...] = x_ref[2304:2496, :].astype(F32)
        for n in range(3):
            tail = x_ref[2496 + n * 16 : 2512 + n * 16, :].astype(F32)
            head32[:, n * 128 : n * 128 + 128] = tail[:4]
            gain32[n * 128 : n * 128 + 128] = tail[4]
        copies.append(copy(1, small.at[0:128, :], g_in.at[:, 0:128]))
        copies.append(copy(2, small.at[128:192, :], g_in.at[0:64, 128:256]))
        copies.append(copy(3, head32, g_head))
        copies.append(copy(4, gain32, g_gain))
        for one in copies:
            one.wait()

    @pl.when(half == 1)
    def _():
        fill(0)
        copies = [copy(0, big.at[:, 0:384], g_qkv.at[:, 768:1152])]
        fill(1)
        copies.append(copy(1, big.at[:, 384:768], g_out))
        small[...] = x_ref[2304:2496, :].astype(F32)
        copies.append(copy(2, small.at[0:64, :], g_in.at[64:128, 128:256]))
        copies.append(copy(3, small.at[64:192, :], g_in.at[:, 256:384]))
        for one in copies:
            one.wait()


def unpack(is_other, x, done=()):
    hbm = pl.BlockSpec(memory_space=pl.ANY)
    shapes = ((128, HID), (HID,), (HID, 3 * HID), (HID, HID), (4, HID))
    return pl.pallas_call(
        functools.partial(unpack_kernel, is_other),
        out_shape=tuple(jax.ShapeDtypeStruct(shape, F32) for shape in shapes),
        in_specs=[pl.BlockSpec(memory_space=pltpu.VMEM)] + [hbm] * len(done),
        out_specs=(hbm,) * 5,
        scratch_shapes=[
            pltpu.VMEM((HID, 2 * HID), F32),
            pltpu.VMEM((192, 128), F32),
            pltpu.VMEM((4, HID), F32),
            pltpu.VMEM((HID,), F32),
            pltpu.SemaphoreType.DMA((5,)),
        ],
        input_output_aliases={i + 1: i for i in range(len(done))},
        compiler_params=pltpu.CompilerParams(vmem_limit_bytes=12 << 20),
        cost_estimate=pl.CostEstimate(flops=0, transcendentals=0, bytes_accessed=2 << 20),
        name="unpack_other" if is_other else "unpack_own",
    )(x, *done)


AXES = ("dp", "frame")
PARTNER = [(i, i ^ 1) for i in range(8)]


def make_groups(mesh):
    nx = max(mesh.shape["dp"] // 8, 1)
    nz = mesh.shape["dp"] // nx
    at = lambda x, y, z, c: (x * nz + z) * 8 + y * 2 + c
    plane = [[at(x, y, z, c) for y in range(4) for x in range(nx)] for z in range(nz) for c in range(2)]
    line = [[at(x, y, z, c) for z in range(nz)] for x in range(nx) for y in range(4) for c in range(2)]
    return plane, line


def swap(x, axis, groups=None):
    return lax.all_to_all(
        x, axis, split_axis=0, concat_axis=0, axis_index_groups=groups, tiled=True
    )


def fold(x, n):
    return jnp.sum(x.reshape(n, x.shape[0] // n, x.shape[1]).astype(F32), axis=0).astype(BF16)


def sum_all(keep, send, groups):
    plane, line = groups
    n, m = len(plane[0]), len(line[0])
    x = (keep.astype(F32) + lax.ppermute(send, "frame", PARTNER).astype(F32)).astype(BF16)
    x = fold(swap(x, AXES, plane), n)
    x = fold(swap(jnp.tile(x, (m, 1)), AXES, line), m)
    x = swap(jnp.tile(x, (n, 1)), AXES, plane)
    return x, lax.ppermute(x, "frame", PARTNER)


def body(
    groups,
    features,
    vis_block,
    vis_count,
    query_frame,
    query_block,
    query_cell,
    cotangent,
    w_in,
    gain,
    w_qkv,
    w_out,
    w_head,
):
    outgoing = gather(vis_block, vis_count, query_frame, query_block, query_cell, features)
    arrived = [
        lax.ppermute(outgoing[s], "frame", [(i, i ^ s) for i in range(8)]) if s else outgoing[0]
        for s in ORDER
    ]
    ct = cotangent[0].reshape(4, 4, 8, 16).transpose(0, 1, 3, 2).reshape(4, TOK)
    ct = jnp.pad(ct, ((0, 12), (0, 0)))
    keep, send = token_grads(
        arrived,
        ct,
        jnp.concatenate([w_in, w_head, jnp.zeros((12, HID), BF16)]),
        gain.reshape(1, HID),
        w_qkv.T,
        w_qkv,
        w_out,
    )
    own, other = sum_all(keep, send, groups)
    return unpack(True, other, unpack(False, own))


def solution(mesh):
    in_specs = (
        P("dp", "frame", None, None, None),
        P("dp", None, "frame", None),
        P("dp", None, "frame"),
        P("dp", None),
        P("dp", None),
        P("dp", None),
        P("dp", None, "frame", None),
        P(),
        P(),
        P(),
        P(),
        P(),
    )
    out_specs = (P(), P(), P(), P(), P())
    step = functools.partial(body, make_groups(mesh))
    return jax.shard_map(step, mesh=mesh, in_specs=in_specs, out_specs=out_specs, check_vma=False)
```

```python
import functools

import jax
import jax.numpy as jnp
from jax import lax
from jax.experimental import pallas as pl
from jax.experimental.pallas import tpu as pltpu
from jax.sharding import PartitionSpec as P

HEADS = 8
SIZE = 48
HID = 384
TOK = 512
ORDER = (4, 5, 2, 3, 6, 7, 1, 0)
HALF = 2560
F32 = jnp.float32
BF16 = jnp.bfloat16


def dot(left, right, dims=((1,), (0,))):
    return lax.dot_general(left, right, (dims, ((), ())), preferred_element_type=F32)


NT = ((1,), (1,))
TN = ((0,), (0,))


def gather_kernel(vis_ref, count_ref, qf_ref, qb_ref, qc_ref, feats_ref, *refs):
    outs, query_ref = refs[:8], refs[8]
    frame = lax.axis_index("frame")
    for s, out_ref in enumerate(outs):
        for gl in range(2):
            g = (frame ^ s) * 2 + gl
            for fr in range(2):
                shown = count_ref[0, fr, g]
                for k in range(2):
                    at = (gl * 2 + fr) * 128 + k * 64
                    tile = feats_ref[0, fr, vis_ref[0, fr, k, g]]
                    if k:
                        tile = jnp.where(shown > k, tile, jnp.zeros_like(tile))
                    out_ref[at : at + 64, :] = tile
    local = qf_ref[...] - frame * 2
    index = local * 2048 + qb_ref[...] * 64 + qc_ref[...]
    index = jnp.where((local >= 0) & (local < 2), index, -1)
    column = jnp.broadcast_to(index, (128, 256)).T[:, :1]
    query = jnp.zeros((256, 128), F32)
    for j in range(8):
        lanes = lax.broadcasted_iota(jnp.int32, (256, 512), 1) + j * 512
        chosen = jnp.where(lanes == column, 1.0, 0.0).astype(BF16)
        rows = feats_ref[0, j // 4, (j % 4) * 8 : (j % 4) * 8 + 8].reshape(512, 128)
        query = query + dot(chosen, rows)
    query_ref[...] = query.astype(BF16).reshape(8, 32, 128)
    for s, out_ref in enumerate(outs):
        out_ref[512:544, :] = query_ref[frame ^ s]


def gather(vis_block, vis_count, query_frame, query_block, query_cell, features):
    vm = pl.BlockSpec(memory_space=pltpu.VMEM)
    sm = pl.BlockSpec(memory_space=pltpu.SMEM)
    return pl.pallas_call(
        gather_kernel,
        out_shape=(jax.ShapeDtypeStruct((544, 128), BF16),) * 8,
        in_specs=[sm, sm, vm, vm, vm, vm],
        out_specs=(vm,) * 8,
        scratch_shapes=[pltpu.VMEM((8, 32, 128), BF16)],
        name="gather",
    )(
        vis_block.transpose(0, 2, 3, 1),
        vis_count.transpose(0, 2, 1),
        query_frame,
        query_block,
        query_cell,
        features,
    )


def token_kernel(*refs):
    token_body(refs[:8], *refs[8:])


def token_body(
    pieces,
    ct_ref,
    w_ends,
    gain_in,
    w_qkv_t,
    w_qkv,
    w_out,
    keep_ref,
    send_ref,
    corr32,
    corr16,
    x_zero,
    normed,
    left,
    qkv,
    d_y,
    d_mixed,
    right,
    inv_ref,
    g_in_ref,
    gain_ref,
    s_ref,
    t_ref,
    p_ref,
    d_ref,
):
    hidden, mixed = left.at[0], left.at[1]
    d_qkv, d_y16 = right.at[0:1152], right.at[1152:1536]
    frame = lax.axis_index("frame")
    core = frame % 2
    gain_ref[...] = jnp.broadcast_to(gain_in[...], (128, HID)).T
    query = sum(ref[512:544, :].astype(F32) for ref in pieces).astype(BF16)
    scale = 128 ** (-0.5)
    for s, ref in zip(ORDER, pieces):
        first = pl.multiple_of((frame ^ s) * 16, 16)
        for g in range(2):
            part = dot(query[g * 16 : g * 16 + 16], ref[g * 256 : g * 256 + 256], NT) * scale
            for half in range(2):
                for fr in range(2):
                    row = pl.multiple_of(first + (g * 2 + half) * 128 + fr * 8, 8)
                    corr32[pl.ds(row, 8), :] = part[
                        half * 8 : half * 8 + 8, fr * 128 : fr * 128 + 128
                    ]
    corr16[...] = corr32[...].astype(BF16)

    ct = ct_ref[...]
    gain = gain_ref[...]
    for c in range(2):
        wide = slice(c * 256, c * 256 + 256)
        dy = dot(w_ends[128:144, :], ct[:, wide], TN)
        d_y[:, wide] = dy
        d_y16[:, wide] = dy.astype(BF16)
        d_mixed[:, wide] = dot(w_out[...], d_y16[:, wide]).astype(BF16)
        x_zero[:, wide] = dot(w_ends[0:128, :], corr16[wide, :], ((0,), (1,)))
        for n in range(2):
            cols = slice(c * 256 + n * 128, c * 256 + n * 128 + 128)
            x0 = x_zero[:, cols]
            centred = x0 - jnp.mean(x0, axis=0, keepdims=True)
            inv = lax.rsqrt(jnp.mean(centred * centred, axis=0, keepdims=True) + 1e-05)
            inv_ref[:, cols] = jnp.broadcast_to(inv, (8, 128))
            nrm = centred * inv
            normed[:, cols] = nrm
            hidden[:, cols] = (nrm * gain).astype(BF16)
        for r in range(3):
            rows = slice(r * 384, r * 384 + 384)
            qkv[rows, wide] = dot(w_qkv_t[rows, :], hidden[:, wide]).astype(BF16)

    own = (
        lax.broadcasted_iota(jnp.int32, (8, 128), 0)
        == lax.broadcasted_iota(jnp.int32, (8, 128), 1) % 8
    ).astype(F32)
    a_scale = SIZE ** (-0.5)
    e_scale = a_scale * 1.4426950408889634

    def block(b, carry):
        def cols(h):
            return slice(h // HEADS * 128, h // HEADS * 128 + 128)

        def rows(h, n):
            at = n * HID + h % HEADS * SIZE
            return slice(at, at + SIZE)

        def scores(h):
            s_ref[h] = dot(qkv[rows(h, 1), cols(h)], qkv[rows(h, 0), cols(h)], TN)
            t_ref[h] = dot(qkv[rows(h, 2), cols(h)], d_mixed[rows(h, 0), cols(h)], TN).astype(BF16)

        def weights(h):
            score = s_ref[h].reshape(16, 8, 128)
            expo = jnp.exp2((score - jnp.max(score, axis=0, keepdims=True)) * e_scale)
            prob = expo * (own / jnp.sum(expo, axis=0))[None]
            p_ref[h] = prob.reshape(128, 128).astype(BF16)
            d_p = t_ref[h].astype(F32).reshape(16, 8, 128)
            inner = jnp.sum(d_p * prob, axis=0, keepdims=True)
            d_ref[h] = (prob * (d_p - inner)).reshape(128, 128).astype(BF16)

        def products(h):
            prob, d_s = p_ref[h], d_ref[h]
            mixed[rows(h, 0), cols(h)] = dot(qkv[rows(h, 2), cols(h)], prob).astype(BF16)
            d_v = dot(d_mixed[rows(h, 0), cols(h)], prob, NT)
            d_q = dot(qkv[rows(h, 1), cols(h)], d_s) * a_scale
            d_k = dot(qkv[rows(h, 0), cols(h)], d_s, NT) * a_scale
            d_qkv[rows(h, 0), cols(h)] = d_q.astype(BF16)
            d_qkv[rows(h, 1), cols(h)] = d_k.astype(BF16)
            d_qkv[rows(h, 2), cols(h)] = d_v.astype(BF16)

        for h in range(4 * HEADS + 4):
            if h < 4 * HEADS:
                scores(h)
            if 2 <= h < 4 * HEADS + 2:
                weights(h - 2)
            if h >= 4:
                products(h - 4)
        return carry

    block(0, 0)

    def pair_grads(ref, half, i):
        j = half * 2 + i
        rows = pl.ds(pl.multiple_of(j * HID, HID), HID)
        part = dot(left[jnp.where(j == 3, 1, 0)], right[rows, :], NT)
        for n in range(3):
            at = (i * 3 + n) * HID
            ref[at : at + HID, :] = part[:, n * 128 : n * 128 + 128].astype(BF16)

    head = jnp.zeros((16, HID), F32)
    gain_sum = jnp.zeros((HID, 128), F32)
    for c in range(2):
        wide = slice(c * 256, c * 256 + 256)
        y16 = (x_zero[:, wide] + dot(w_out[...], mixed[:, wide], TN)).astype(BF16)
        head = head + dot(ct[:, wide], y16, NT)
        x_zero[:, wide] = dot(w_qkv[...], d_qkv[:, wide])
        for n in range(2):
            cols = slice(c * 256 + n * 128, c * 256 + n * 128 + 128)
            pair_grads(*((send_ref, 1 - core, n), (keep_ref, core, n))[c])
            dh, nrm = x_zero[:, cols], normed[:, cols]
            gain_sum = gain_sum + dh * nrm
            dn = dh * gain
            m_one = jnp.mean(dn, axis=0, keepdims=True)
            m_two = jnp.mean(dn * nrm, axis=0, keepdims=True)
            dx = inv_ref[:1, cols] * (dn - m_one - nrm * m_two) + d_y[:, cols]
            d_mixed[:, cols] = dx.astype(BF16)
    g_in = dot(corr16[...], d_mixed[...], ((0,), (1,)))
    gain_row = jnp.sum(gain_sum.T, axis=0, keepdims=True)
    at_four = lax.broadcasted_iota(jnp.int32, (16, HID), 0) == 4
    head = jnp.where(at_four, jnp.broadcast_to(gain_row, (16, HID)), head)
    for j in range(3):
        g_in_ref[j * 128 : j * 128 + 128, :] = g_in[:, j * 128 : j * 128 + 128]
    for ref, half in ((keep_ref, core), (send_ref, 1 - core)):
        ref[2304:2496, :] = g_in_ref[pl.ds(pl.multiple_of(half * 192, 8), 192), :].astype(BF16)
        part = jnp.where(half == 0, head, 0.0).astype(BF16)
        for n in range(3):
            ref[2496 + n * 16 : 2512 + n * 16, :] = part[:, n * 128 : n * 128 + 128]
        ref[2544:HALF, :] = jnp.zeros((HALF - 2544, 128), BF16)


def token_grads(pieces, ct, w_ends, gain, w_qkv_t, w_qkv, w_out):
    vm = pl.BlockSpec(memory_space=pltpu.VMEM)
    half = jax.ShapeDtypeStruct((HALF, 128), BF16)
    return pl.pallas_call(
        token_kernel,
        out_shape=(half, half),
        in_specs=[vm] * 14,
        out_specs=(vm, vm),
        scratch_shapes=[
            pltpu.VMEM((TOK, 128), F32),
            pltpu.VMEM((TOK, 128), BF16),
            pltpu.VMEM((HID, TOK), F32),
            pltpu.VMEM((HID, TOK), F32),
            pltpu.VMEM((2, HID, TOK), BF16),
            pltpu.VMEM((3 * HID, TOK), BF16),
            pltpu.VMEM((HID, TOK), F32),
            pltpu.VMEM((HID, TOK), BF16),
            pltpu.VMEM((4 * HID, TOK), BF16),
            pltpu.VMEM((8, TOK), F32),
            pltpu.VMEM((HID, 128), F32),
            pltpu.VMEM((HID, 128), F32),
            pltpu.VMEM((4 * HEADS, 128, 128), F32),
            pltpu.VMEM((4 * HEADS, 128, 128), BF16),
            pltpu.VMEM((4 * HEADS, 128, 128), BF16),
            pltpu.VMEM((4 * HEADS, 128, 128), BF16),
        ],
        compiler_params=pltpu.CompilerParams(vmem_limit_bytes=28 << 20),
        name="token_grads",
    )(*pieces, ct, w_ends, gain, w_qkv_t, w_qkv, w_out)


def unpack_kernel(is_other, x_ref, *refs):
    g_in, g_gain, g_qkv, g_out, g_head, big, small, head32, gain32, sems = refs[-10:]
    half = lax.axis_index("frame") % 2
    if is_other:
        half = 1 - half

    def fill(j):
        for n in range(3):
            at = (j * 3 + n) * HID
            big[:, j * HID + n * 128 : j * HID + n * 128 + 128] = x_ref[at : at + HID, :].astype(F32)

    def copy(n, source, target):
        one = pltpu.make_async_copy(source, target, sems.at[n])
        one.start()
        return one

    @pl.when(half == 0)
    def _():
        fill(0)
        fill(1)
        copies = [copy(0, big, g_qkv.at[:, 0:768])]
        small[...] = x_ref[2304:2496, :].astype(F32)
        for n in range(3):
            tail = x_ref[2496 + n * 16 : 2512 + n * 16, :].astype(F32)
            head32[:, n * 128 : n * 128 + 128] = tail[:4]
            gain32[n * 128 : n * 128 + 128] = tail[4]
        copies.append(copy(1, small.at[0:128, :], g_in.at[:, 0:128]))
        copies.append(copy(2, small.at[128:192, :], g_in.at[0:64, 128:256]))
        copies.append(copy(3, head32, g_head))
        copies.append(copy(4, gain32, g_gain))
        for one in copies:
            one.wait()

    @pl.when(half == 1)
    def _():
        fill(0)
        copies = [copy(0, big.at[:, 0:384], g_qkv.at[:, 768:1152])]
        fill(1)
        copies.append(copy(1, big.at[:, 384:768], g_out))
        small[...] = x_ref[2304:2496, :].astype(F32)
        copies.append(copy(2, small.at[0:64, :], g_in.at[64:128, 128:256]))
        copies.append(copy(3, small.at[64:192, :], g_in.at[:, 256:384]))
        for one in copies:
            one.wait()


def unpack(is_other, x, done=()):
    hbm = pl.BlockSpec(memory_space=pl.ANY)
    shapes = ((128, HID), (HID,), (HID, 3 * HID), (HID, HID), (4, HID))
    return pl.pallas_call(
        functools.partial(unpack_kernel, is_other),
        out_shape=tuple(jax.ShapeDtypeStruct(shape, F32) for shape in shapes),
        in_specs=[pl.BlockSpec(memory_space=pltpu.VMEM)] + [hbm] * len(done),
        out_specs=(hbm,) * 5,
        scratch_shapes=[
            pltpu.VMEM((HID, 2 * HID), F32),
            pltpu.VMEM((192, 128), F32),
            pltpu.VMEM((4, HID), F32),
            pltpu.VMEM((HID,), F32),
            pltpu.SemaphoreType.DMA((5,)),
        ],
        input_output_aliases={i + 1: i for i in range(len(done))},
        compiler_params=pltpu.CompilerParams(vmem_limit_bytes=12 << 20),
        cost_estimate=pl.CostEstimate(flops=0, transcendentals=0, bytes_accessed=2 << 20),
        name="unpack_other" if is_other else "unpack_own",
    )(x, *done)


AXES = ("dp", "frame")
PARTNER = [(i, i ^ 1) for i in range(8)]


def make_groups(mesh):
    nx = max(mesh.shape["dp"] // 8, 1)
    nz = mesh.shape["dp"] // nx
    at = lambda x, y, z, c: (x * nz + z) * 8 + y * 2 + c
    plane = [[at(x, y, z, c) for y in range(4) for x in range(nx)] for z in range(nz) for c in range(2)]
    line = [[at(x, y, z, c) for z in range(nz)] for x in range(nx) for y in range(4) for c in range(2)]
    return plane, line


def swap(x, axis, groups=None):
    return lax.all_to_all(
        x, axis, split_axis=0, concat_axis=0, axis_index_groups=groups, tiled=True
    )


def fold(x, n):
    return jnp.sum(x.reshape(n, x.shape[0] // n, x.shape[1]).astype(F32), axis=0).astype(BF16)


def sum_all(keep, send, groups):
    plane, line = groups
    n, m = len(plane[0]), len(line[0])
    x = (keep.astype(F32) + lax.ppermute(send, "frame", PARTNER).astype(F32)).astype(BF16)
    x = fold(swap(x, AXES, plane), n)
    x = fold(swap(jnp.tile(x, (m, 1)), AXES, line), m)
    x = swap(jnp.tile(x, (n, 1)), AXES, plane)
    return x, lax.ppermute(x, "frame", PARTNER)


def body(
    groups,
    features,
    vis_block,
    vis_count,
    query_frame,
    query_block,
    query_cell,
    cotangent,
    w_in,
    gain,
    w_qkv,
    w_out,
    w_head,
):
    outgoing = gather(vis_block, vis_count, query_frame, query_block, query_cell, features)
    arrived = [
        lax.ppermute(outgoing[s], "frame", [(i, i ^ s) for i in range(8)]) if s else outgoing[0]
        for s in ORDER
    ]
    ct = cotangent[0].reshape(4, 4, 8, 16).transpose(0, 1, 3, 2).reshape(4, TOK)
    ct = jnp.pad(ct, ((0, 12), (0, 0)))
    keep, send = token_grads(
        arrived,
        ct,
        jnp.concatenate([w_in, w_head, jnp.zeros((12, HID), BF16)]),
        gain.reshape(1, HID),
        w_qkv.T,
        w_qkv,
        w_out,
    )
    own, other = sum_all(keep, send, groups)
    return unpack(True, other, unpack(False, own))


def solution(mesh):
    in_specs = (
        P("dp", "frame", None, None, None),
        P("dp", None, "frame", None),
        P("dp", None, "frame"),
        P("dp", None),
        P("dp", None),
        P("dp", None),
        P("dp", None, "frame", None),
        P(),
        P(),
        P(),
        P(),
        P(),
    )
    out_specs = (P(), P(), P(), P(), P())
    step = functools.partial(body, make_groups(mesh))
    return jax.shard_map(step, mesh=mesh, in_specs=in_specs, out_specs=out_specs, check_vma=False)
```
